512 devices in a mesh: layer: 128 (over x, z, y_lo), dp: 4 (over y_hi, core).
Axes of the slice: x: 4, y: 8 (y_hi: 2, y_lo: 4; y = y_hi * 4 + y_lo), z: 8, core: 2. Of those that a mesh axis runs over, the one named last changes fastest.
Arguments:
- state_guess: float32 [128, 4, 32, 256], P('layer', 'dp'), may hold values from -6 to 6
- adjoint_guess: float32 [128, 4, 32, 256], P('layer', 'dp'), may hold values from -6 to 6
- conv_weight: bfloat16 [512, 32, 288], P('layer'), may hold values from -0.375 to 0.375
- conv_bias: float32 [512, 32], P('layer'), may hold values from -3 to 3
Outputs:
- state_fixed: float32 [128, 4, 32, 256], P('layer', 'dp')
- adjoint_fixed: float32 [128, 4, 32, 256], P('layer', 'dp')
- weight_grad: float32 [512, 32, 288], P('layer', 'dp')
- bias_grad: float32 [512, 32], P('layer', 'dp')
The draws below stay inside these ranges and needn't reach their ends.
All inputs are finite; a program needn't handle non-finite values.
Results may differ from the reference program's by a relative error of at most 0.0071.
Values sent between devices are 32-bit elements; how exact they have to be, the bound alone decides.
A program may use at most 64 MiB of HBM per device.

```python
import jax
import jax.numpy as jnp
from jax import lax

C = 32
IMG = 16
L_DEV = 4
HW = 256
BATCH = 4
LAYERS = 512
N_LAYER = 128


def level_of(own_key, extent, split, smallest, top_value):
    loudness, own = 1.0, jax.random.fold_in(own_key, 6)
    for axis_at, shards_of in split:
        draws = jnp.exp(jax.random.uniform(jax.random.fold_in(own, axis_at), (shards_of,), jnp.float32, smallest / len(split), top_value / len(split)))
        loudness = loudness * jnp.repeat(draws, extent[axis_at] // shards_of).reshape([-1 if axis == axis_at else 1 for axis in range(len(extent))])
    return loudness


def scatter_about(key, dims, scale, bound, split=(), dtype=jnp.bfloat16):
    loudness = level_of(key, dims, split, -0.22, 0.18) if split else 1.0
    values = jax.random.normal(key, dims, jnp.float32) * scale * loudness
    return jnp.minimum(jnp.maximum(values, -bound), bound).astype(dtype)


def setup_inputs(seed: int = 0) -> dict:
    key_list = jax.random.split(jax.random.key(seed), 5)
    return {
        "state_guess": scatter_about(key_list[0], (N_LAYER, BATCH, C, HW), 1.0, 6.0, ((0, 128), (1, 4)), jnp.float32),
        "adjoint_guess": scatter_about(key_list[1], (N_LAYER, BATCH, C, HW), 1.0, 6.0, ((0, 128), (1, 4)), jnp.float32),
        "conv_weight": scatter_about(key_list[2], (LAYERS, C, 9 * C), (9 * C) ** -0.5, 0.375, ((0, 128),)),
        "conv_bias": scatter_about(key_list[3], (LAYERS, C), 0.5, 3.0, ((0, 128),), jnp.float32),
    }


step_size = 0.5


def gather_taps(values):
    count = values.shape[0]
    grid = values.reshape(count, C, IMG, IMG)
    padded = jnp.pad(grid, ((0, 0), (0, 0), (1, 1), (1, 1)))
    taps = [padded[:, :, row:row + IMG, col:col + IMG] for row in range(3) for col in range(3)]
    return jnp.stack(taps, axis=2).reshape(count, C * 9, IMG * IMG)


def spread_taps(grads):
    count = grads.shape[0]
    grid = grads.reshape(count, C, 9, IMG, IMG)
    total = jnp.zeros((count, C, IMG + 2, IMG + 2), jnp.float32)
    for tap in range(9):
        row, col = tap // 3, tap % 3
        total = total + jnp.pad(grid[:, :, tap], ((0, 0), (0, 0), (row, 2 - row), (col, 2 - col)))
    return total[:, :, 1:-1, 1:-1].reshape(count, C, IMG * IMG)


def forward_block(state, weights, biases):
    gain = jnp.ones(state.shape, jnp.float32)
    saved = []
    for layer in range(L_DEV):
        kernel = weights[layer]
        rounded = state.astype(jnp.bfloat16)
        patch = gather_taps(rounded)
        pre = jnp.einsum("ok,bkp->bop", kernel.astype(jnp.float32), patch.astype(jnp.float32)) + biases[layer][None, :, None]
        squash = jnp.tanh(pre)
        center = jnp.diagonal(kernel.reshape(C, C, 9)[:, :, 4]).astype(jnp.float32)
        gain = gain * (1.0 + step_size * (1.0 - squash * squash) * center[None, :, None])
        state = state + step_size * squash
        saved.append((rounded, squash))
    return state, gain, saved


def backward_block(adjoint, weights, saved):
    wgrads = []
    bgrads = []
    for layer in reversed(range(L_DEV)):
        rounded, squash = saved[layer]
        kernel = weights[layer]
        dz = step_size * adjoint * (1.0 - squash * squash)
        dzb = dz.astype(jnp.bfloat16)
        back = jnp.einsum("ok,bop->bkp", kernel.astype(jnp.float32), dzb.astype(jnp.float32))
        adjoint = adjoint + spread_taps(back)
        wgrads.append(jnp.einsum("bop,bkp->ok", dzb.astype(jnp.float32), gather_taps(rounded).astype(jnp.float32)))
        bgrads.append(jnp.sum(dz, axis=(0, 2)))
    return adjoint, jnp.stack(wgrads[::-1]), jnp.stack(bgrads[::-1])


def relax_pair(items):
    state, adjoint, weights, biases = items
    final, gain, saved = forward_block(state, weights, biases)
    back, wgrad, bgrad = backward_block(adjoint, weights, saved)
    return final, gain, back


def grad_pass(items):
    state, adjoint, weights, biases = items
    final, gain, saved = forward_block(state, weights, biases)
    back, wgrad, bgrad = backward_block(adjoint, weights, saved)
    return wgrad, bgrad


def reference(state_guess, adjoint_guess, conv_weight, conv_bias):
    weights = conv_weight.reshape(N_LAYER, L_DEV, C, 9 * C)
    biases = conv_bias.reshape(N_LAYER, L_DEV, C)
    final, gain, back = lax.map(relax_pair, (state_guess, adjoint_guess, weights, biases))

    def forward_link(carry, items):
        gain_prev, final_prev, guess = items
        fresh = gain_prev * carry + final_prev - guess
        return fresh, fresh

    zero = jnp.zeros(state_guess.shape[1:], jnp.float32)
    _, fwd_err = lax.scan(forward_link, zero, (gain[:-1], final[:-1], state_guess[1:]))
    state_fixed = jnp.concatenate([state_guess[:1], state_guess[1:] + fwd_err], axis=0)
    _, bwd_err = lax.scan(forward_link, zero, (gain[1:], back[1:], adjoint_guess[:-1]), reverse=True)
    adjoint_fixed = jnp.concatenate([adjoint_guess[:-1] + bwd_err, adjoint_guess[-1:]], axis=0)
    wgrad, bgrad = lax.map(grad_pass, (state_guess, adjoint_fixed, weights, biases))
    return state_fixed, adjoint_fixed, wgrad.reshape(LAYERS, C, 9 * C), bgrad.reshape(LAYERS, C)
```

```python
import jax
import jax.numpy as jnp
from jax import lax
from jax.experimental import pallas as pl
from jax.experimental.pallas import tpu as pltpu
from jax.sharding import Mesh
from jax.sharding import PartitionSpec as P

IMG = 16
HW = 256
C = 32
L = 4
ROWS = 3 * C
LAYER = ("layer_0", "layer_1", "layer_2")
F32 = jnp.float32
BF16 = jnp.bfloat16


def shifted(x, axis, by):
    length = lax.axis_size(axis)
    pairs = [(i, i + by) for i in range(length) if 0 <= i + by < length]
    return lax.ppermute(x, axis, pairs)


def nothing_yet(x, identity):
    return jax.tree.map(
        lambda part, zero: jnp.zeros_like(part) + jnp.asarray(zero, part.dtype), x, identity
    )


def gathered_once(x, axis):
    both = lax.all_gather(jnp.concatenate(x, axis=0), axis)
    return tuple(both[:, k * C : (k + 1) * C] for k in range(len(x)))


def entering(x, axes, combine, identity, reverse):
    before = start = nothing_yet(x, identity)
    total = x
    for axis in reversed(axes):
        length, here = (lax.axis_size(axis), lax.axis_index(axis))
        pieces = gathered_once(total, axis)
        inside, total = (start, start)
        for k in reversed(range(length)) if reverse else range(length):
            passed = k > here if reverse else k < here
            total = combine(total, jax.tree.map(lambda part: part[k], pieces))
            inside = jax.tree.map(lambda new, old: jnp.where(passed, new, old), total, inside)
        before = combine(inside, before)
    return before


def compose(earlier, later):
    return (later[0] * earlier[0], later[0] * earlier[1] + later[1])


def shift_x(v, by):
    at = lax.broadcasted_iota(jnp.int32, v.shape, 1) & (IMG - 1)
    keep = (at < IMG - 1) if by > 0 else (at > 0)
    return jnp.where(keep, pltpu.roll(v, (-by) % HW, 1), 0.0)


def shift_y(v, by):
    at = lax.broadcasted_iota(jnp.int32, v.shape, 1)
    keep = (at < HW - IMG) if by > 0 else (at >= IMG)
    return jnp.where(keep, pltpu.roll(v, (-IMG * by) % HW, 1), 0.0)


def order_table():
    row = lax.broadcasted_iota(jnp.int32, (9 * C, 384), 0)
    col = lax.broadcasted_iota(jnp.int32, (9 * C, 384), 1)
    dy, rest = col >> 7, col & 127
    want = (rest & (C - 1)) * 9 + 3 * dy + (rest >> 5)
    return jnp.where((row == want) & (rest < ROWS), 1.0, 0.0).astype(BF16)


def column_of(row):
    eye = lax.broadcasted_iota(jnp.int32, (C, C), 0) == lax.broadcasted_iota(jnp.int32, (C, C), 1)
    return jnp.sum(jnp.where(eye, jnp.broadcast_to(row, (C, C)), 0.0), axis=1, keepdims=True)


def prepare(weights, mats, mats_t):
    wide = jnp.dot(weights, order_table(), preferred_element_type=F32)
    centers = []
    pad = jnp.zeros((128 - ROWS, 128), F32)
    for n in range(L):
        part = [wide[n * C : (n + 1) * C, dy * 128 : (dy + 1) * 128] for dy in range(3)]
        full = jnp.concatenate(part + [pad], axis=0)
        mats[n] = full[:ROWS].astype(BF16)
        mats_t[n] = full.T[:ROWS].astype(BF16)
        at = lax.broadcasted_iota(jnp.int32, (C, 128), 1)
        want = lax.broadcasted_iota(jnp.int32, (C, 128), 0) + C
        centers.append(jnp.sum(jnp.where(at == want, part[1], 0.0), axis=1, keepdims=True))
    return centers


def forward_layer(state, mat, bias, center, gain):
    taps = jnp.concatenate([shift_x(state, -1), state, shift_x(state, 1)], axis=0).astype(BF16)
    prod = jnp.dot(mat[:, :ROWS], taps, preferred_element_type=F32)
    pre = shift_y(prod[:C], -1) + prod[C : 2 * C] + shift_y(prod[2 * C :], 1) + bias
    squash = jnp.tanh(pre)
    slope = 0.5 * (1.0 - squash * squash)
    return state + 0.5 * squash, gain * (1.0 + slope * center), taps, slope


def spread(dz):
    return jnp.concatenate([shift_y(dz, 1), dz, shift_y(dz, -1)], axis=0).astype(BF16)


def backward_layer(adjoint, mat_t, wide):
    prod = jnp.dot(mat_t[:, :ROWS], wide, preferred_element_type=F32)
    return adjoint + (shift_x(prod[:C], 1) + prod[C : 2 * C] + shift_x(prod[2 * C :], -1))


def relax_kernel(u_ref, a_ref, w_ref, b_ref, final_ref, gain_ref, back_ref, taps_ref, slope_ref, mats_t, mats):
    centers = prepare(w_ref[...], mats, mats_t)
    state, gain = u_ref[...], jnp.ones((C, HW), F32)
    for n in range(L):
        bias = column_of(b_ref[n : n + 1, :])
        state, gain, taps, slope = forward_layer(state, mats[n], bias, centers[n], gain)
        taps_ref[n] = taps
        slope_ref[n] = slope
    final_ref[...] = state
    gain_ref[...] = gain
    adjoint = a_ref[...]
    for n in reversed(range(L)):
        adjoint = backward_layer(adjoint, mats_t[n], spread(adjoint * slope_ref[n]))
    back_ref[...] = adjoint


def grad_kernel(a_ref, taps_ref, slope_ref, mats_t, part_ref):
    adjoint = a_ref[...]
    lane = lax.broadcasted_iota(jnp.int32, (C, 128), 1)
    for n in reversed(range(L)):
        dz = adjoint * slope_ref[n]
        wide = spread(dz)
        grad = lax.dot_general(
            wide, taps_ref[n], (((1,), (1,)), ((), ())), preferred_element_type=F32
        )
        grad = jnp.concatenate([grad, jnp.zeros((ROWS, 128 - ROWS), F32)], axis=1)
        sums = jnp.sum(dz, axis=1, keepdims=True)
        for dy in range(3):
            here = grad[dy * C : (dy + 1) * C]
            if dy == 1:
                here = jnp.where(lane == ROWS, sums, here)
            for owner in range(4):
                part_ref[owner, n, dy] = here[owner * 8 : (owner + 1) * 8]
        if n > 0:
            adjoint = backward_layer(adjoint, mats_t[n], wide)


def exact_dot_t(x, table):
    total = None
    for _ in range(3):
        part = x.astype(BF16)
        x = x - part.astype(F32)
        term = lax.dot_general(part, table, (((1,), (1,)), ((), ())), preferred_element_type=F32)
        total = term if total is None else total + term
    return total


def finish(total, wg_ref, bg_ref):
    rows = jnp.concatenate([jnp.concatenate(total[n], axis=1) for n in range(L)], axis=0)
    grads = exact_dot_t(rows, order_table())
    eye = lax.broadcasted_iota(jnp.int32, (8, 8), 0) == lax.broadcasted_iota(jnp.int32, (8, 8), 1)
    for n in range(L):
        wg_ref[n] = grads[n * 8 : (n + 1) * 8]
        col = total[n][1][:, ROWS : ROWS + 1]
        row = jnp.sum(jnp.where(eye, jnp.broadcast_to(col, (8, 8)), 0.0), axis=0, keepdims=True)
        bg_ref[n : n + 1, :] = row


def finish_kernel(parts_ref, wg_ref, bg_ref):
    total = [
        [
            (parts_ref[0, n, dy] + parts_ref[1, n, dy]) + (parts_ref[2, n, dy] + parts_ref[3, n, dy])
            for dy in range(3)
        ]
        for n in range(L)
    ]
    finish(total, wg_ref, bg_ref)


def relax(start, guess_adj, weights, biases):
    grid = jax.ShapeDtypeStruct((C, HW), F32)
    return pl.pallas_call(
        relax_kernel,
        out_shape=(
            grid, grid, grid,
            jax.ShapeDtypeStruct((L, ROWS, HW), BF16),
            jax.ShapeDtypeStruct((L, C, HW), F32),
            jax.ShapeDtypeStruct((L, ROWS, 128), BF16),
        ),
        scratch_shapes=[pltpu.VMEM((L, ROWS, 128), BF16)],
    )(start, guess_adj, weights, biases)


def grads_of(adjoint, taps, slopes, mats_t):
    return pl.pallas_call(
        grad_kernel, out_shape=jax.ShapeDtypeStruct((4, L, 3, 8, 128), F32)
    )(adjoint, taps, slopes, mats_t)


def finished(parts):
    return pl.pallas_call(
        finish_kernel,
        out_shape=(
            jax.ShapeDtypeStruct((L, 8, 9 * C), F32),
            jax.ShapeDtypeStruct((L, 8), F32),
        ),
    )(parts)


def local(state_guess, adjoint_guess, conv_weight, conv_bias):
    start = state_guess[0, 0]
    guess_adj = adjoint_guess[0, 0]
    next_guess = shifted(start, LAYER, -1)
    prev_guess = shifted(guess_adj, LAYER, 1)
    final, gain, back, taps, slopes, mats_t = relax(
        start, guess_adj, conv_weight.reshape(L * C, 9 * C), conv_bias
    )
    one, zero = jnp.ones(start.shape, F32), jnp.zeros(start.shape, F32)
    fwd_pre = entering((gain, final - next_guess), LAYER, compose, (one, zero), False)
    bwd_pre = entering((gain, back - prev_guess), LAYER, compose, (one, zero), True)
    state_fixed = start + fwd_pre[1]
    adjoint_fixed = guess_adj + bwd_pre[1]
    parts = grads_of(adjoint_fixed, taps, slopes, mats_t)
    weight_grad, bias_grad = finished(lax.all_to_all(parts, "dp", 0, 0, tiled=True))
    return (state_fixed[None, None], adjoint_fixed[None, None], weight_grad, bias_grad)


def solution(mesh):
    torus = Mesh(
        mesh.devices.reshape(4, 8, 4, mesh.shape["dp"]), ("layer_0", "layer_1", "layer_2", "dp")
    )
    return jax.shard_map(
        local,
        mesh=torus,
        in_specs=(
            P(LAYER, "dp", None, None),
            P(LAYER, "dp", None, None),
            P(LAYER, None, None),
            P(LAYER, None),
        ),
        out_specs=(
            P(LAYER, "dp", None, None),
            P(LAYER, "dp", None, None),
            P(LAYER, "dp", None),
            P(LAYER, "dp"),
        ),
        check_vma=False,
    )
```

```python
import jax
import jax.numpy as jnp
from jax import lax
from jax.experimental import pallas as pl
from jax.experimental.pallas import tpu as pltpu
from jax.sharding import Mesh
from jax.sharding import PartitionSpec as P

IMG = 16
HW = 256
C = 32
L = 4
ROWS = 3 * C
LAYER = ("x", "z", "y")
DP = ("h", "c")
MESH = pl.DeviceIdType.MESH
F32 = jnp.float32
BF16 = jnp.bfloat16


def shift_x(v, by):
    at = lax.broadcasted_iota(jnp.int32, v.shape, 1) & (IMG - 1)
    keep = (at < IMG - 1) if by > 0 else (at > 0)
    return jnp.where(keep, pltpu.roll(v, (-by) % HW, 1), 0.0)


def shift_y(v, by):
    at = lax.broadcasted_iota(jnp.int32, v.shape, 1)
    keep = (at < HW - IMG) if by > 0 else (at >= IMG)
    return jnp.where(keep, pltpu.roll(v, (-IMG * by) % HW, 1), 0.0)


def order_table():
    row = lax.broadcasted_iota(jnp.int32, (9 * C, 384), 0)
    col = lax.broadcasted_iota(jnp.int32, (9 * C, 384), 1)
    dy, rest = col >> 7, col & 127
    want = (rest & (C - 1)) * 9 + 3 * dy + (rest >> 5)
    return jnp.where((row == want) & (rest < ROWS), 1.0, 0.0).astype(BF16)


def column_of(row):
    eye = lax.broadcasted_iota(jnp.int32, (C, C), 0) == lax.broadcasted_iota(jnp.int32, (C, C), 1)
    return jnp.sum(jnp.where(eye, jnp.broadcast_to(row, (C, C)), 0.0), axis=1, keepdims=True)


def prepare(weights, mats, mats_t):
    wide = jnp.dot(weights, order_table(), preferred_element_type=F32)
    centers = []
    pad = jnp.zeros((128 - ROWS, 128), F32)
    for n in range(L):
        part = [wide[n * C : (n + 1) * C, dy * 128 : (dy + 1) * 128] for dy in range(3)]
        full = jnp.concatenate(part + [pad], axis=0)
        mats[n] = full[:ROWS].astype(BF16)
        mats_t[n] = full.T[:ROWS].astype(BF16)
        at = lax.broadcasted_iota(jnp.int32, (C, 128), 1)
        want = lax.broadcasted_iota(jnp.int32, (C, 128), 0) + C
        centers.append(jnp.sum(jnp.where(at == want, part[1], 0.0), axis=1, keepdims=True))
    return centers


def forward_layer(state, mat, bias, center, gain):
    taps = jnp.concatenate([shift_x(state, -1), state, shift_x(state, 1)], axis=0).astype(BF16)
    prod = jnp.dot(mat[:, :ROWS], taps, preferred_element_type=F32)
    pre = shift_y(prod[:C], -1) + prod[C : 2 * C] + shift_y(prod[2 * C :], 1) + bias
    squash = jnp.tanh(pre)
    slope = 0.5 * (1.0 - squash * squash)
    return state + 0.5 * squash, gain * (1.0 + slope * center), taps, slope


def spread(dz):
    return jnp.concatenate([shift_y(dz, 1), dz, shift_y(dz, -1)], axis=0).astype(BF16)


def backward_layer(adjoint, mat_t, wide):
    prod = jnp.dot(mat_t[:, :ROWS], wide, preferred_element_type=F32)
    return adjoint + (shift_x(prod[:C], 1) + prod[C : 2 * C] + shift_x(prod[2 * C :], -1))


def exact_dot_t(x, table):
    total = None
    for _ in range(3):
        part = x.astype(BF16)
        x = x - part.astype(F32)
        term = lax.dot_general(part, table, (((1,), (1,)), ((), ())), preferred_element_type=F32)
        total = term if total is None else total + term
    return total


def finish(total, wg_ref, bg_ref):
    rows = jnp.concatenate([jnp.concatenate(total[n], axis=1) for n in range(L)], axis=0)
    grads = exact_dot_t(rows, order_table())
    eye = lax.broadcasted_iota(jnp.int32, (8, 8), 0) == lax.broadcasted_iota(jnp.int32, (8, 8), 1)
    for n in range(L):
        wg_ref[n] = grads[n * 8 : (n + 1) * 8]
        col = total[n][1][:, ROWS : ROWS + 1]
        row = jnp.sum(jnp.where(eye, jnp.broadcast_to(col, (8, 8)), 0.0), axis=0, keepdims=True)
        bg_ref[n : n + 1, :] = row


def send(src, dst, sems, slot, device):
    copy = pltpu.make_async_remote_copy(
        src_ref=src,
        dst_ref=dst,
        send_sem=sems[0].at[slot],
        recv_sem=sems[1].at[slot],
        device_id=device,
        device_id_type=MESH,
    )
    copy.start()
    return copy


def total_of(parts):
    gain, fwd, _ = parts[0]
    for g, r, _ in parts[1:]:
        gain, fwd = gain * g, g * fwd + r
    bwd = parts[-1][2]
    for g, _, s in reversed(parts[:-1]):
        bwd = g * bwd + s
    return gain, fwd, bwd


def entering_all(parts, fwd, bwd):
    fwds, bwds = [fwd], [bwd]
    for g, r, _ in parts[:-1]:
        fwds.append(g * fwds[-1] + r)
    for g, _, s in reversed(parts[1:]):
        bwds.insert(0, g * bwds[0] + s)
    return fwds, bwds


def chosen(values, here):
    out = values[0]
    for k in range(1, len(values)):
        out = jnp.where(here == k, values[k], out)
    return out


def cycle_kernel(
    u_ref, a_ref, w_ref, b_ref,
    state_ref, adj_ref, wg_ref, bg_ref,
    mats, mats_t, taps_ref, slope_ref,
    next_u, prev_a, y_out, y_in, z_out, z_in, x_out, x_in, e_out, e_in,
    c_out, c_in, h_out, h_in,
    n_s, n_r, y_s, y_r, z_s, z_r, x_s, x_r, e_s, e_r, c_s, c_r, h_s, h_r,
):
    x, z, y = lax.axis_index("x"), lax.axis_index("z"), lax.axis_index("y")
    h, c = lax.axis_index("h"), lax.axis_index("c")
    nx, nz, ny = lax.axis_size("x"), lax.axis_size("z"), lax.axis_size("y")
    count = nx * nz * ny
    me = (x * nz + z) * ny + y

    def at(j):
        return {"x": lax.div(j, nz * ny), "z": lax.rem(lax.div(j, ny), nz), "y": lax.rem(j, ny)}

    after, before = at(lax.rem(me + 1, count)), at(lax.rem(me + count - 1, count))
    ys = [lax.rem(y + k, ny) for k in range(ny)]
    zs = [lax.rem(z + k, nz) for k in range(nz)]
    xs = [lax.rem(x + k, nx) for k in range(nx)]
    partners = [after, before]
    partners += [{"y": q} for q in ys[1:]] + [{"z": q} for q in zs[1:]] + [{"x": q} for q in xs[1:]]
    partners += [{"c": 1 - c}, {"h": 1 - h}]
    barrier = pltpu.get_barrier_semaphore()
    for who in partners:
        pl.semaphore_signal(barrier, inc=1, device_id=who, device_id_type=MESH)

    centers = prepare(w_ref[...], mats, mats_t)
    pl.semaphore_wait(barrier, len(partners))
    to_before = send(u_ref, next_u, (n_s, n_r), 0, before)
    to_after = send(a_ref, prev_a, (n_s, n_r), 1, after)

    state, gain = u_ref[...], jnp.ones((C, HW), F32)
    for n in range(L):
        bias = column_of(b_ref[n : n + 1, :])
        state, gain, taps, slope = forward_layer(state, mats[n], bias, centers[n], gain)
        taps_ref[n] = taps
        slope_ref[n] = slope
    adjoint = a_ref[...]
    for n in reversed(range(L)):
        adjoint = backward_layer(adjoint, mats_t[n], spread(adjoint * slope_ref[n]))

    to_before.wait()
    to_after.wait()
    fwd = state - next_u[...]
    bwd = adjoint - prev_a[...]
    for q in range(ny):
        y_out[q, 0] = gain[q * 8 : q * 8 + 8]
        y_out[q, 1] = fwd[q * 8 : q * 8 + 8]
        y_out[q, 2] = bwd[q * 8 : q * 8 + 8]
    copies = [send(y_out.at[ys[k]], y_in.at[y], (y_s, y_r), k, {"y": ys[k]}) for k in range(1, ny)]
    y_in[y] = y_out[y]
    for copy in copies:
        copy.wait()
    y_parts = [tuple(y_in[k, i] for i in range(3)) for k in range(ny)]
    for i, part in enumerate(total_of(y_parts)):
        z_out[i] = part
    copies = [send(z_out, z_in.at[z], (z_s, z_r), k, {"z": zs[k]}) for k in range(1, nz)]
    z_in[z] = z_out[...]
    for copy in copies:
        copy.wait()
    z_parts = [tuple(z_in[k, i] for i in range(3)) for k in range(nz)]
    for i, part in enumerate(total_of(z_parts)):
        x_out[i] = part
    copies = [send(x_out, x_in.at[x], (x_s, x_r), k, {"x": xs[k]}) for k in range(1, nx)]
    x_in[x] = x_out[...]
    for copy in copies:
        copy.wait()
    x_parts = [tuple(x_in[k, i] for i in range(3)) for k in range(nx)]
    zero = jnp.zeros((8, HW), F32)
    es, fs = entering_all(x_parts, zero, zero)
    es, fs = entering_all(z_parts, chosen(es, x), chosen(fs, x))
    es, fs = entering_all(y_parts, chosen(es, z), chosen(fs, z))
    for q in range(ny):
        e_out[q, 0] = es[q]
        e_out[q, 1] = fs[q]
    copies = [send(e_out.at[ys[k]], e_in.at[y], (e_s, e_r), k, {"y": ys[k]}) for k in range(1, ny)]
    e_in[y] = e_out[y]
    for copy in copies:
        copy.wait()
    adjoint = a_ref[...] + jnp.concatenate([e_in[q, 1] for q in range(ny)], axis=0)
    adj_ref[...] = adjoint
    state_ref[...] = u_ref[...] + jnp.concatenate([e_in[q, 0] for q in range(ny)], axis=0)

    lane = lax.broadcasted_iota(jnp.int32, (C, 128), 1)
    mine = {}

    def over_cores(n):
        to_core[n].wait()
        h_out[n] = c_out[c, 1 - h, n] + c_in[1 - h, n]
        mine[n] = [c_out[c, h, n, dy] + c_in[h, n, dy] for dy in range(3)]
        return send(h_out.at[n], h_in.at[n], (h_s, h_r), n, {"h": 1 - h})

    to_core, to_far = {}, {}
    for n in reversed(range(L)):
        dz = adjoint * slope_ref[n]
        wide = spread(dz)
        grad = lax.dot_general(
            wide, taps_ref[n], (((1,), (1,)), ((), ())), preferred_element_type=F32
        )
        grad = jnp.concatenate([grad, jnp.zeros((ROWS, 128 - ROWS), F32)], axis=1)
        sums = jnp.sum(dz, axis=1, keepdims=True)
        for dy in range(3):
            here = grad[dy * C : (dy + 1) * C]
            if dy == 1:
                here = jnp.where(lane == ROWS, sums, here)
            for owner in range(4):
                c_out[owner % 2, owner // 2, n, dy] = here[owner * 8 : (owner + 1) * 8]
        to_core[n] = send(
            c_out.at[1 - c, :, n], c_in.at[:, n], (c_s, c_r), n, {"c": 1 - c}
        )
        if n > 0:
            adjoint = backward_layer(adjoint, mats_t[n], wide)
        if n < L - 1:
            to_far[n + 1] = over_cores(n + 1)
    to_far[0] = over_cores(0)
    for n in reversed(range(L)):
        to_far[n].wait()
    finish([[mine[n][dy] + h_in[n, dy] for dy in range(3)] for n in range(L)], wg_ref, bg_ref)


def local(state_guess, adjoint_guess, conv_weight, conv_bias):
    grid = jax.ShapeDtypeStruct((C, HW), F32)
    nx, nz, ny = (lax.axis_size(axis) for axis in LAYER)
    dma = pltpu.SemaphoreType.DMA
    tile = (3, 8, HW)
    state_fixed, adjoint_fixed, weight_grad, bias_grad = pl.pallas_call(
        cycle_kernel,
        out_shape=(
            grid,
            grid,
            jax.ShapeDtypeStruct((L, 8, 9 * C), F32),
            jax.ShapeDtypeStruct((L, 8), F32),
        ),
        in_specs=[pl.BlockSpec(memory_space=pltpu.VMEM)] * 4,
        out_specs=tuple([pl.BlockSpec(memory_space=pltpu.VMEM)] * 4),
        scratch_shapes=[
            pltpu.VMEM((L, ROWS, 128), BF16),
            pltpu.VMEM((L, ROWS, 128), BF16),
            pltpu.VMEM((L, ROWS, HW), BF16),
            pltpu.VMEM((L, C, HW), F32),
            pltpu.VMEM((C, HW), F32),
            pltpu.VMEM((C, HW), F32),
            pltpu.VMEM((ny, *tile), F32),
            pltpu.VMEM((ny, *tile), F32),
            pltpu.VMEM(tile, F32),
            pltpu.VMEM((nz, *tile), F32),
            pltpu.VMEM(tile, F32),
            pltpu.VMEM((nx, *tile), F32),
            pltpu.VMEM((ny, 2, 8, HW), F32),
            pltpu.VMEM((ny, 2, 8, HW), F32),
            pltpu.VMEM((2, 2, L, 3, 8, 128), F32),
            pltpu.VMEM((2, L, 3, 8, 128), F32),
            pltpu.VMEM((L, 3, 8, 128), F32),
            pltpu.VMEM((L, 3, 8, 128), F32),
            dma((2,)), dma((2,)),
            dma((ny,)), dma((ny,)),
            dma((nz,)), dma((nz,)),
            dma((nx,)), dma((nx,)),
            dma((ny,)), dma((ny,)),
            dma((L,)), dma((L,)),
            dma((L,)), dma((L,)),
        ],
        compiler_params=pltpu.CompilerParams(collective_id=0, has_side_effects=True),
    )(
        state_guess.reshape(C, HW),
        adjoint_guess.reshape(C, HW),
        conv_weight.reshape(L * C, 9 * C),
        conv_bias,
    )
    return (state_fixed[None, None], adjoint_fixed[None, None], weight_grad, bias_grad)


def solution(mesh):
    across = mesh.shape["layer"] // 32
    torus = Mesh(mesh.devices.reshape(across, 8, 4, 2, mesh.shape["dp"] // 2), (*LAYER, *DP))
    return jax.shard_map(
        local,
        mesh=torus,
        in_specs=(
            P(LAYER, DP, None, None),
            P(LAYER, DP, None, None),
            P(LAYER, None, None),
            P(LAYER, None),
        ),
        out_specs=(
            P(LAYER, DP, None, None),
            P(LAYER, DP, None, None),
            P(LAYER, DP, None),
            P(LAYER, DP),
        ),
        check_vma=False,
    )
```

```python
import jax
import jax.numpy as jnp
from jax import lax
from jax.experimental import pallas as pl
from jax.experimental.pallas import tpu as pltpu
from jax.sharding import Mesh
from jax.sharding import PartitionSpec as P

IMG = 16
HW = 256
C = 32
L = 4
ROWS = 3 * C
LAYER = ("x", "z", "y")
DP = ("h", "c")
MESH = pl.DeviceIdType.MESH
F32 = jnp.float32
BF16 = jnp.bfloat16


def shift_x(v, by):
    at = lax.broadcasted_iota(jnp.int32, v.shape, 1) & (IMG - 1)
    keep = (at < IMG - 1) if by > 0 else (at > 0)
    return jnp.where(keep, pltpu.roll(v, (-by) % HW, 1), 0.0)


def shift_y(v, by):
    at = lax.broadcasted_iota(jnp.int32, v.shape, 1)
    keep = (at < HW - IMG) if by > 0 else (at >= IMG)
    return jnp.where(keep, pltpu.roll(v, (-IMG * by) % HW, 1), 0.0)


def order_table():
    row = lax.broadcasted_iota(jnp.int32, (9 * C, 384), 0)
    col = lax.broadcasted_iota(jnp.int32, (9 * C, 384), 1)
    dy, rest = col >> 7, col & 127
    want = (rest & (C - 1)) * 9 + 3 * dy + (rest >> 5)
    return jnp.where((row == want) & (rest < ROWS), 1.0, 0.0).astype(BF16)


def column_of(row):
    eye = lax.broadcasted_iota(jnp.int32, (C, C), 0) == lax.broadcasted_iota(jnp.int32, (C, C), 1)
    return jnp.sum(jnp.where(eye, jnp.broadcast_to(row, (C, C)), 0.0), axis=1, keepdims=True)


def prepare(weights, mats, mats_t):
    wide = jnp.dot(weights, order_table(), preferred_element_type=F32)
    centers = []
    pad = jnp.zeros((128 - ROWS, 128), F32)
    for n in range(L):
        part = [wide[n * C : (n + 1) * C, dy * 128 : (dy + 1) * 128] for dy in range(3)]
        full = jnp.concatenate(part + [pad], axis=0)
        mats[n] = full[:ROWS].astype(BF16)
        mats_t[n] = full.T[:ROWS].astype(BF16)
        at = lax.broadcasted_iota(jnp.int32, (C, 128), 1)
        want = lax.broadcasted_iota(jnp.int32, (C, 128), 0) + C
        centers.append(jnp.sum(jnp.where(at == want, part[1], 0.0), axis=1, keepdims=True))
    return centers


def forward_layer(state, mat, bias, center, gain):
    taps = jnp.concatenate([shift_x(state, -1), state, shift_x(state, 1)], axis=0).astype(BF16)
    prod = jnp.dot(mat[:, :ROWS], taps, preferred_element_type=F32)
    pre = shift_y(prod[:C], -1) + prod[C : 2 * C] + shift_y(prod[2 * C :], 1) + bias
    squash = jnp.tanh(pre)
    slope = 0.5 * (1.0 - squash * squash)
    return state + 0.5 * squash, gain * (1.0 + slope * center), taps, slope


def spread(dz):
    return jnp.concatenate([shift_y(dz, 1), dz, shift_y(dz, -1)], axis=0).astype(BF16)


def backward_layer(adjoint, mat_t, wide):
    prod = jnp.dot(mat_t[:, :ROWS], wide, preferred_element_type=F32)
    return adjoint + (shift_x(prod[:C], 1) + prod[C : 2 * C] + shift_x(prod[2 * C :], -1))


def exact_dot_t(x, table):
    total = None
    for _ in range(3):
        part = x.astype(BF16)
        x = x - part.astype(F32)
        term = lax.dot_general(part, table, (((1,), (1,)), ((), ())), preferred_element_type=F32)
        total = term if total is None else total + term
    return total


def finish(total, wg_ref, bg_ref):
    rows = jnp.concatenate([jnp.concatenate(total[n], axis=1) for n in range(L)], axis=0)
    grads = exact_dot_t(rows, order_table())
    eye = lax.broadcasted_iota(jnp.int32, (8, 8), 0) == lax.broadcasted_iota(jnp.int32, (8, 8), 1)
    for n in range(L):
        wg_ref[n] = grads[n * 8 : (n + 1) * 8]
        col = total[n][1][:, ROWS : ROWS + 1]
        row = jnp.sum(jnp.where(eye, jnp.broadcast_to(col, (8, 8)), 0.0), axis=0, keepdims=True)
        bg_ref[n : n + 1, :] = row


def send(src, dst, sems, slot, device):
    copy = pltpu.make_async_remote_copy(
        src_ref=src,
        dst_ref=dst,
        send_sem=sems[0].at[slot],
        recv_sem=sems[1].at[slot],
        device_id=device,
        device_id_type=MESH,
    )
    copy.start()
    return copy


def chained(gains, adds, start):
    values = [start]
    for g, r in zip(gains, adds):
        values.append(r if values[-1] is None else g * values[-1] + r)
    return values


def chosen(values, here):
    out = values[0]
    for k in range(1, len(values)):
        out = jnp.where(here == k, values[k], out)
    return out


def product(values):
    out = values[0]
    for v in values[1:]:
        out = out * v
    return out


def cycle_kernel(
    u_ref, a_ref, w_ref, b_ref,
    state_ref, adj_ref, sum_ref,
    mats, mats_t, taps_ref, slope_ref,
    ua_out, ua_in, gf_out, gf_in, s_out, s_in, z_out, z_in, x_out, x_in, e_out, e_in,
    c_out, c_in, h_out, h_in,
    y_s, y_r, z_s, z_r, x_s, x_r, c_s, c_r, h_s, h_r,
):
    x, z, y = lax.axis_index("x"), lax.axis_index("z"), lax.axis_index("y")
    h, c = lax.axis_index("h"), lax.axis_index("c")
    nx, nz, ny = lax.axis_size("x"), lax.axis_size("z"), lax.axis_size("y")
    ys = [lax.rem(y + k, ny) for k in range(ny)]
    zs = [lax.rem(z + k, nz) for k in range(nz)]
    xs = [lax.rem(x + k, nx) for k in range(nx)]
    partners = [{"y": q} for q in ys[1:]] + [{"z": q} for q in zs[1:]] + [{"x": q} for q in xs[1:]]
    partners += [{"c": 1 - c}, {"h": 1 - h}]
    barrier = pltpu.get_barrier_semaphore()
    for who in partners:
        pl.semaphore_signal(barrier, inc=1, device_id=who, device_id_type=MESH)

    def along_y(out, into, kind):
        copies = [
            send(out.at[ys[k]], into.at[y], (y_s.at[kind], y_r.at[kind]), k, {"y": ys[k]})
            for k in range(1, ny)
        ]
        into[y] = out[y]
        return copies

    def along_z(kind, value):
        z_out[kind] = value
        copies = [
            send(z_out.at[kind], z_in.at[kind, z], (z_s.at[kind], z_r.at[kind]), k, {"z": zs[k]})
            for k in range(1, nz)
        ]
        z_in[kind, z] = value
        return copies

    def along_x(kind, value):
        x_out[kind] = value
        copies = [
            send(x_out.at[kind], x_in.at[kind, x], (x_s.at[kind], x_r.at[kind]), k, {"x": xs[k]})
            for k in range(1, nx)
        ]
        x_in[kind, x] = value
        return copies

    def landed(copies):
        for copy in copies:
            copy.wait()

    for q in range(ny):
        ua_out[q, 0] = u_ref[q * 8 : q * 8 + 8]
        ua_out[q, 1] = a_ref[q * 8 : q * 8 + 8]
    centers = prepare(w_ref[...], mats, mats_t)
    pl.semaphore_wait(barrier, len(partners))
    ua_copies = along_y(ua_out, ua_in, 0)

    state, gain = u_ref[...], jnp.ones((C, HW), F32)
    for n in range(L):
        bias = column_of(b_ref[n : n + 1, :])
        state, gain, taps, slope = forward_layer(state, mats[n], bias, centers[n], gain)
        taps_ref[n] = taps
        slope_ref[n] = slope
    for q in range(ny):
        gf_out[q, 0] = gain[q * 8 : q * 8 + 8]
        gf_out[q, 1] = state[q * 8 : q * 8 + 8]
    gf_copies = along_y(gf_out, gf_in, 1)
    adjoint = a_ref[...]
    for n in reversed(range(L)):
        adjoint = backward_layer(adjoint, mats_t[n], spread(adjoint * slope_ref[n]))
    for q in range(ny):
        s_out[q] = adjoint[q * 8 : q * 8 + 8]
    s_copies = along_y(s_out, s_in, 2)

    first = (x == 0) & (z == 0)
    last = (x == nx - 1) & (z == nz - 1)
    zero = jnp.zeros((8, HW), F32)
    G, S, R = 0, 1, 2
    landed(ua_copies)
    landed(gf_copies)
    guess = [ua_in[k, 0] for k in range(ny)]
    guess_adj = [ua_in[k, 1] for k in range(ny)]
    gains = [gf_in[k, 0] for k in range(ny)]
    finals = [gf_in[k, 1] for k in range(ny)]
    zg = along_z(G, jnp.where(first | last, 0.0, product(gains)))
    f_adds = [finals[k] - guess[k + 1] for k in range(ny - 1)] + [finals[ny - 1]]
    leaves = chained(gains, f_adds, jnp.where(first, 0.0, -guess[0]))[ny]
    landed(s_copies)
    backs = [s_in[k] for k in range(ny)]
    b_adds = [backs[k] - guess_adj[k - 1] for k in range(ny - 1, 0, -1)] + [backs[0]]
    zs_ = along_z(S, chained(gains[::-1], b_adds, jnp.where(last, 0.0, -guess_adj[ny - 1]))[ny])
    zr = along_z(R, leaves)

    landed(zg)
    z_gain = [z_in[G, k] for k in range(nz)]
    xg = along_x(G, product(z_gain))
    landed(zs_)
    z_bwd = [z_in[S, k] for k in range(nz)][::-1]
    xs_ = along_x(S, chained(z_gain[::-1], z_bwd, None)[nz])
    landed(zr)
    z_fwd = [z_in[R, k] for k in range(nz)]
    xr = along_x(R, chained(z_gain, z_fwd, None)[nz])

    landed(xg)
    x_gain = [x_in[G, k] for k in range(nx)]
    landed(xs_)
    x_bwd = [x_in[S, k] for k in range(nx)][::-1]
    came = chosen(chained(x_gain[::-1], x_bwd, zero)[:nx][::-1], x)
    came = chosen(chained(z_gain[::-1], z_bwd, came)[:nz][::-1], z)
    fs = chained(gains[::-1], b_adds, jnp.where(last, 0.0, came - guess_adj[ny - 1]))[:ny][::-1]
    for q in range(ny):
        e_out[0, q] = fs[q]
    f_copies = along_y(e_out.at[0], e_in.at[0], 3)
    landed(xr)
    x_fwd = [x_in[R, k] for k in range(nx)]
    came = chosen(chained(x_gain, x_fwd, zero)[:nx], x)
    came = chosen(chained(z_gain, z_fwd, came)[:nz], z)
    es = chained(gains, f_adds, jnp.where(first, 0.0, came - guess[0]))[:ny]
    for q in range(ny):
        e_out[1, q] = es[q]
    e_copies = along_y(e_out.at[1], e_in.at[1], 4)
    landed(f_copies)
    adjoint = a_ref[...] + jnp.concatenate([e_in[0, q] for q in range(ny)], axis=0)
    adj_ref[...] = adjoint

    lane = lax.broadcasted_iota(jnp.int32, (C, 128), 1)
    mine = {}

    def over_cores(n):
        to_core[n].wait()
        h_out[n] = c_out[c, 1 - h, n] + c_in[1 - h, n]
        mine[n] = [c_out[c, h, n, dy] + c_in[h, n, dy] for dy in range(3)]
        return send(h_out.at[n], h_in.at[n], (h_s, h_r), n, {"h": 1 - h})

    to_core, to_far = {}, {}
    for n in reversed(range(L)):
        dz = adjoint * slope_ref[n]
        wide = spread(dz)
        grad = lax.dot_general(
            wide, taps_ref[n], (((1,), (1,)), ((), ())), preferred_element_type=F32
        )
        grad = jnp.concatenate([grad, jnp.zeros((ROWS, 128 - ROWS), F32)], axis=1)
        sums = jnp.sum(dz, axis=1, keepdims=True)
        for dy in range(3):
            here = grad[dy * C : (dy + 1) * C]
            if dy == 1:
                here = jnp.where(lane == ROWS, sums, here)
            for owner in range(4):
                c_out[owner % 2, owner // 2, n, dy] = here[owner * 8 : (owner + 1) * 8]
        to_core[n] = send(
            c_out.at[1 - c, :, n], c_in.at[:, n], (c_s, c_r), n, {"c": 1 - c}
        )
        if n > 0:
            adjoint = backward_layer(adjoint, mats_t[n], wide)
        if n < L - 1:
            to_far[n + 1] = over_cores(n + 1)
    to_far[0] = over_cores(0)
    landed(e_copies)
    state_ref[...] = u_ref[...] + jnp.concatenate([e_in[1, q] for q in range(ny)], axis=0)
    for n in reversed(range(L)):
        to_far[n].wait()
        for dy in range(3):
            sum_ref[n, dy] = mine[n][dy] + h_in[n, dy]


def finish_kernel(state_ref, adj_ref, sum_ref, state_out, adj_out, wg_ref, bg_ref):
    state_out[...] = state_ref[...]
    adj_out[...] = adj_ref[...]
    finish([[sum_ref[n, dy] for dy in range(3)] for n in range(L)], wg_ref, bg_ref)


def local(state_guess, adjoint_guess, conv_weight, conv_bias):
    grid = jax.ShapeDtypeStruct((C, HW), F32)
    nx, nz, ny = (lax.axis_size(axis) for axis in LAYER)
    dma = pltpu.SemaphoreType.DMA
    rows = (8, HW)
    results = pl.pallas_call(
        cycle_kernel,
        out_shape=(grid, grid, jax.ShapeDtypeStruct((L, 3, 8, 128), F32)),
        in_specs=[pl.BlockSpec(memory_space=pltpu.VMEM)] * 4,
        out_specs=tuple([pl.BlockSpec(memory_space=pltpu.VMEM)] * 3),
        scratch_shapes=[
            pltpu.VMEM((L, ROWS, 128), BF16),
            pltpu.VMEM((L, ROWS, 128), BF16),
            pltpu.VMEM((L, ROWS, HW), BF16),
            pltpu.VMEM((L, C, HW), F32),
            pltpu.VMEM((ny, 2, *rows), F32),
            pltpu.VMEM((ny, 2, *rows), F32),
            pltpu.VMEM((ny, 2, *rows), F32),
            pltpu.VMEM((ny, 2, *rows), F32),
            pltpu.VMEM((ny, *rows), F32),
            pltpu.VMEM((ny, *rows), F32),
            pltpu.VMEM((3, *rows), F32),
            pltpu.VMEM((3, nz, *rows), F32),
            pltpu.VMEM((3, *rows), F32),
            pltpu.VMEM((3, nx, *rows), F32),
            pltpu.VMEM((2, ny, *rows), F32),
            pltpu.VMEM((2, ny, *rows), F32),
            pltpu.VMEM((2, 2, L, 3, 8, 128), F32),
            pltpu.VMEM((2, L, 3, 8, 128), F32),
            pltpu.VMEM((L, 3, 8, 128), F32),
            pltpu.VMEM((L, 3, 8, 128), F32),
            dma((5, ny)), dma((5, ny)),
            dma((3, nz)), dma((3, nz)),
            dma((3, nx)), dma((3, nx)),
            dma((L,)), dma((L,)),
            dma((L,)), dma((L,)),
        ],
        compiler_params=pltpu.CompilerParams(collective_id=0, has_side_effects=True),
    )(
        state_guess.reshape(C, HW),
        adjoint_guess.reshape(C, HW),
        conv_weight.reshape(L * C, 9 * C),
        conv_bias,
    )
    state_fixed, adjoint_fixed, weight_grad, bias_grad = pl.pallas_call(
        finish_kernel,
        out_shape=(
            grid,
            grid,
            jax.ShapeDtypeStruct((L, 8, 9 * C), F32),
            jax.ShapeDtypeStruct((L, 8), F32),
        ),
    )(*results)
    return (state_fixed[None, None], adjoint_fixed[None, None], weight_grad, bias_grad)


def solution(mesh):
    across = mesh.shape["layer"] // 32
    torus = Mesh(mesh.devices.reshape(across, 8, 4, 2, mesh.shape["dp"] // 2), (*LAYER, *DP))
    return jax.shard_map(
        local,
        mesh=torus,
        in_specs=(
            P(LAYER, DP, None, None),
            P(LAYER, DP, None, None),
            P(LAYER, None, None),
            P(LAYER, None),
        ),
        out_specs=(
            P(LAYER, DP, None, None),
            P(LAYER, DP, None, None),
            P(LAYER, DP, None),
            P(LAYER, DP),
        ),
        check_vma=False,
    )
```

```python
import jax
import jax.numpy as jnp
from jax import lax
from jax.experimental import pallas as pl
from jax.experimental.pallas import tpu as pltpu
from jax.sharding import Mesh
from jax.sharding import PartitionSpec as P

IMG = 16
HW = 256
C = 32
L = 4
ROWS = 3 * C
LAYER = ("x", "z", "y")
DP = ("h", "c")
MESH = pl.DeviceIdType.MESH
F32 = jnp.float32
BF16 = jnp.bfloat16


def shift_x(v, by):
    at = lax.broadcasted_iota(jnp.int32, v.shape, 1) & (IMG - 1)
    keep = (at < IMG - 1) if by > 0 else (at > 0)
    return jnp.where(keep, pltpu.roll(v, (-by) % HW, 1), 0.0)


def shift_y(v, by):
    at = lax.broadcasted_iota(jnp.int32, v.shape, 1)
    keep = (at < HW - IMG) if by > 0 else (at >= IMG)
    return jnp.where(keep, pltpu.roll(v, (-IMG * by) % HW, 1), 0.0)


def order_table():
    row = lax.broadcasted_iota(jnp.int32, (9 * C, 384), 0)
    col = lax.broadcasted_iota(jnp.int32, (9 * C, 384), 1)
    dy, rest = col >> 7, col & 127
    want = (rest & (C - 1)) * 9 + 3 * dy + (rest >> 5)
    return jnp.where((row == want) & (rest < ROWS), 1.0, 0.0).astype(BF16)


def column_of(row):
    eye = lax.broadcasted_iota(jnp.int32, (C, C), 0) == lax.broadcasted_iota(jnp.int32, (C, C), 1)
    return jnp.sum(jnp.where(eye, jnp.broadcast_to(row, (C, C)), 0.0), axis=1, keepdims=True)


def prepare(weights, table, mats, mats_t):
    wide = jnp.dot(weights, table, preferred_element_type=F32)
    centers = []
    pad = jnp.zeros((128 - ROWS, 128), F32)
    for n in range(L):
        part = [wide[n * C : (n + 1) * C, dy * 128 : (dy + 1) * 128] for dy in range(3)]
        full = jnp.concatenate(part + [pad], axis=0)
        mats[n] = full[:ROWS].astype(BF16)
        mats_t[n] = full.T[:ROWS].astype(BF16)
        at = lax.broadcasted_iota(jnp.int32, (C, 128), 1)
        want = lax.broadcasted_iota(jnp.int32, (C, 128), 0) + C
        centers.append(jnp.sum(jnp.where(at == want, part[1], 0.0), axis=1, keepdims=True))
    return centers


def forward_layer(state, mat, bias, center, gain):
    taps = jnp.concatenate([shift_x(state, -1), state, shift_x(state, 1)], axis=0).astype(BF16)
    prod = jnp.dot(mat[:, :ROWS], taps, preferred_element_type=F32)
    pre = shift_y(prod[:C], -1) + prod[C : 2 * C] + shift_y(prod[2 * C :], 1) + bias
    squash = jnp.tanh(pre)
    slope = 0.5 * (1.0 - squash * squash)
    return state + 0.5 * squash, gain * (1.0 + slope * center), taps, slope


def spread(dz):
    return jnp.concatenate([shift_y(dz, 1), dz, shift_y(dz, -1)], axis=0).astype(BF16)


def backward_layer(adjoint, mat_t, wide):
    prod = jnp.dot(mat_t[:, :ROWS], wide, preferred_element_type=F32)
    return adjoint + (shift_x(prod[:C], 1) + prod[C : 2 * C] + shift_x(prod[2 * C :], -1))


def exact_dot_t(x, table):
    total = None
    for _ in range(3):
        part = x.astype(BF16)
        x = x - part.astype(F32)
        term = lax.dot_general(part, table, (((1,), (1,)), ((), ())), preferred_element_type=F32)
        total = term if total is None else total + term
    return total


def finish(total, table, wg_ref, bg_ref):
    rows = jnp.concatenate([jnp.concatenate(total[n], axis=1) for n in range(L)], axis=0)
    grads = exact_dot_t(rows, table)
    eye = lax.broadcasted_iota(jnp.int32, (8, 8), 0) == lax.broadcasted_iota(jnp.int32, (8, 8), 1)
    for n in range(L):
        wg_ref[n] = grads[n * 8 : (n + 1) * 8]
        col = total[n][1][:, ROWS : ROWS + 1]
        row = jnp.sum(jnp.where(eye, jnp.broadcast_to(col, (8, 8)), 0.0), axis=0, keepdims=True)
        bg_ref[n : n + 1, :] = row


def send(src, dst, sems, slot, device):
    copy = pltpu.make_async_remote_copy(
        src_ref=src,
        dst_ref=dst,
        send_sem=sems[0].at[slot],
        recv_sem=sems[1].at[slot],
        device_id=device,
        device_id_type=MESH,
    )
    copy.start()
    return copy


def chained(gains, adds, start):
    values = [start]
    for g, r in zip(gains, adds):
        values.append(r if values[-1] is None else g * values[-1] + r)
    return values


def chosen(values, here):
    out = values[0]
    for k in range(1, len(values)):
        out = jnp.where(here == k, values[k], out)
    return out


def product(values):
    out = values[0]
    for v in values[1:]:
        out = out * v
    return out


def cycle_kernel(
    u_hbm, a_hbm, w_hbm, b_hbm,
    state_ref, adj_ref, sum_ref,
    u_ref, a_ref, w_ref, b_ref, in_sems, table,
    mats, mats_t, taps_ref, slope_ref,
    yc_out, yc_in, yr_out, yr_in, zc_out, zc_in, zr_out, zr_in, xc_out, xc_in, xr_out, xr_in,
    e_out, e_in, c_out, c_in, h_out, h_in,
    y_s, y_r, z_s, z_r, x_s, x_r, c_s, c_r, h_s, h_r,
):
    x, z, y = lax.axis_index("x"), lax.axis_index("z"), lax.axis_index("y")
    h, c = lax.axis_index("h"), lax.axis_index("c")
    nx, nz, ny = lax.axis_size("x"), lax.axis_size("z"), lax.axis_size("y")
    ys = [lax.rem(y + k, ny) for k in range(ny)]
    zs = [lax.rem(z + k, nz) for k in range(nz)]
    xs = [lax.rem(x + k, nx) for k in range(nx)]
    partners = [{"y": q} for q in ys[1:]] + [{"z": q} for q in zs[1:]] + [{"x": q} for q in xs[1:]]
    partners += [{"c": 1 - c}, {"h": 1 - h}]
    barrier = pltpu.get_barrier_semaphore()
    for who in partners:
        pl.semaphore_signal(barrier, inc=1, device_id=who, device_id_type=MESH)

    inputs = [
        pltpu.make_async_copy(src, dst, in_sems.at[k])
        for k, (src, dst) in enumerate(
            [(w_hbm, w_ref), (b_hbm, b_ref), (u_hbm, u_ref), (a_hbm, a_ref)]
        )
    ]
    for copy in inputs:
        copy.start()

    def gather(axis, here, others, out, into, sems, own):
        copies = [
            send(out if own else out.at[q], into.at[here], sems, k + 1, {axis: q})
            for k, q in enumerate(others)
        ]
        into[here] = out[...] if own else out[here]
        return copies

    def along_y(kind, out, into):
        return gather("y", y, ys[1:], out, into, (y_s.at[kind], y_r.at[kind]), False)

    def along_z(kind, out, into):
        return gather("z", z, zs[1:], out, into, (z_s.at[kind], z_r.at[kind]), True)

    def along_x(kind, out, into):
        return gather("x", x, xs[1:], out, into, (x_s.at[kind], x_r.at[kind]), True)

    def landed(copies):
        for copy in copies:
            copy.wait()

    table[...] = order_table()
    landed(inputs)
    centers = prepare(w_ref[...], table[...], mats, mats_t)
    state, gain = u_ref[...], jnp.ones((C, HW), F32)
    for n in range(L):
        bias = column_of(b_ref[n : n + 1, :])
        state, gain, taps, slope = forward_layer(state, mats[n], bias, centers[n], gain)
        taps_ref[n] = taps
        slope_ref[n] = slope
    adjoint = a_ref[...]
    for n in reversed(range(L)):
        adjoint = backward_layer(adjoint, mats_t[n], spread(adjoint * slope_ref[n]))
    for q in range(ny):
        rows = slice(q * 8, q * 8 + 8)
        yc_out[q, 0] = a_ref[rows]
        yc_out[q, 1] = gain[rows]
        yc_out[q, 2] = adjoint[rows]
        yr_out[q, 0] = u_ref[rows]
        yr_out[q, 1] = state[rows]
    pl.semaphore_wait(barrier, len(partners))
    yc = along_y(0, yc_out, yc_in)
    yr = along_y(1, yr_out, yr_in)

    first = (x == 0) & (z == 0)
    last = (x == nx - 1) & (z == nz - 1)
    zero = jnp.zeros((8, HW), F32)
    landed(yc)
    guess_adj = [yc_in[k, 0] for k in range(ny)]
    gains = [yc_in[k, 1] for k in range(ny)]
    backs = [yc_in[k, 2] for k in range(ny)]
    b_adds = [backs[k] - guess_adj[k - 1] for k in range(ny - 1, 0, -1)] + [backs[0]]
    zc_out[0] = jnp.where(first | last, 0.0, product(gains))
    zc_out[1] = chained(gains[::-1], b_adds, jnp.where(last, 0.0, -guess_adj[ny - 1]))[ny]
    zc = along_z(0, zc_out, zc_in)
    landed(yr)
    guess = [yr_in[k, 0] for k in range(ny)]
    finals = [yr_in[k, 1] for k in range(ny)]
    f_adds = [finals[k] - guess[k + 1] for k in range(ny - 1)] + [finals[ny - 1]]
    zr_out[...] = chained(gains, f_adds, jnp.where(first, 0.0, -guess[0]))[ny]

    landed(zc)
    z_gain = [zc_in[k, 0] for k in range(nz)]
    z_bwd = [zc_in[k, 1] for k in range(nz)][::-1]
    xc_out[0] = product(z_gain)
    xc_out[1] = chained(z_gain[::-1], z_bwd, None)[nz]
    xc = along_x(0, xc_out, xc_in)
    zr = along_z(1, zr_out, zr_in)

    landed(xc)
    x_gain = [xc_in[k, 0] for k in range(nx)]
    x_bwd = [xc_in[k, 1] for k in range(nx)][::-1]
    came = chosen(chained(x_gain[::-1], x_bwd, zero)[:nx][::-1], x)
    came = chosen(chained(z_gain[::-1], z_bwd, came)[:nz][::-1], z)
    fs = chained(gains[::-1], b_adds, jnp.where(last, 0.0, came - guess_adj[ny - 1]))[:ny][::-1]
    for q in range(ny):
        e_out[0, q] = fs[q]
    f_copies = along_y(2, e_out.at[0], e_in.at[0])
    landed(zr)
    z_fwd = [zr_in[k] for k in range(nz)]
    xr_out[...] = chained(z_gain, z_fwd, None)[nz]
    xr = along_x(1, xr_out, xr_in)
    landed(f_copies)
    adjoint = a_ref[...] + jnp.concatenate([e_in[0, q] for q in range(ny)], axis=0)
    adj_ref[...] = adjoint

    def state_rows():
        landed(xr)
        x_fwd = [xr_in[k] for k in range(nx)]
        came = chosen(chained(x_gain, x_fwd, zero)[:nx], x)
        came = chosen(chained(z_gain, z_fwd, came)[:nz], z)
        es = chained(gains, f_adds, jnp.where(first, 0.0, came - guess[0]))[:ny]
        for q in range(ny):
            e_out[1, q] = es[q]
        return along_y(3, e_out.at[1], e_in.at[1])

    lane = lax.broadcasted_iota(jnp.int32, (C, 128), 1)
    mine = {}

    def over_cores(n):
        to_core[n].wait()
        h_out[n] = c_out[c, 1 - h, n] + c_in[1 - h, n]
        mine[n] = [c_out[c, h, n, dy] + c_in[h, n, dy] for dy in range(3)]
        return send(h_out.at[n], h_in.at[n], (h_s, h_r), n, {"h": 1 - h})

    to_core, to_far = {}, {}
    for n in reversed(range(L)):
        dz = adjoint * slope_ref[n]
        wide = spread(dz)
        grad = lax.dot_general(
            wide, taps_ref[n], (((1,), (1,)), ((), ())), preferred_element_type=F32
        )
        grad = jnp.concatenate([grad, jnp.zeros((ROWS, 128 - ROWS), F32)], axis=1)
        sums = jnp.sum(dz, axis=1, keepdims=True)
        for dy in range(3):
            here = grad[dy * C : (dy + 1) * C]
            if dy == 1:
                here = jnp.where(lane == ROWS, sums, here)
            for owner in range(4):
                c_out[owner % 2, owner // 2, n, dy] = here[owner * 8 : (owner + 1) * 8]
        to_core[n] = send(
            c_out.at[1 - c, :, n], c_in.at[:, n], (c_s, c_r), n, {"c": 1 - c}
        )
        if n > 0:
            adjoint = backward_layer(adjoint, mats_t[n], wide)
        if n == L - 2:
            e_copies = state_rows()
        if n < L - 2:
            to_far[n + 2] = over_cores(n + 2)
    for n in (1, 0):
        to_far[n] = over_cores(n)
    landed(e_copies)
    state_ref[...] = u_ref[...] + jnp.concatenate([e_in[1, q] for q in range(ny)], axis=0)
    for n in reversed(range(L)):
        to_far[n].wait()
        for dy in range(3):
            sum_ref[n, dy] = mine[n][dy] + h_in[n, dy]


def finish_kernel(state_ref, adj_ref, sum_ref, state_out, adj_out, wg_ref, bg_ref, sums, table, sems):
    copies = [
        pltpu.make_async_copy(src, dst, sems.at[k])
        for k, (src, dst) in enumerate(
            [(sum_ref, sums), (state_ref, state_out), (adj_ref, adj_out)]
        )
    ]
    for copy in copies:
        copy.start()
    table[...] = order_table()
    copies[0].wait()
    finish([[sums[n, dy] for dy in range(3)] for n in range(L)], table[...], wg_ref, bg_ref)
    for copy in copies[1:]:
        copy.wait()


def local(state_guess, adjoint_guess, conv_weight, conv_bias):
    grid = jax.ShapeDtypeStruct((C, HW), F32)
    nx, nz, ny = (lax.axis_size(axis) for axis in LAYER)
    dma = pltpu.SemaphoreType.DMA
    rows = (8, HW)
    results = pl.pallas_call(
        cycle_kernel,
        out_shape=(grid, grid, jax.ShapeDtypeStruct((L, 3, 8, 128), F32)),
        in_specs=[pl.BlockSpec(memory_space=pltpu.HBM)] * 4,
        out_specs=tuple([pl.BlockSpec(memory_space=pltpu.VMEM)] * 3),
        scratch_shapes=[
            pltpu.VMEM((C, HW), F32),
            pltpu.VMEM((C, HW), F32),
            pltpu.VMEM((L * C, 9 * C), BF16),
            pltpu.VMEM((L, C), F32),
            dma((4,)),
            pltpu.VMEM((9 * C, 384), BF16),
            pltpu.VMEM((L, ROWS, 128), BF16),
            pltpu.VMEM((L, ROWS, 128), BF16),
            pltpu.VMEM((L, ROWS, HW), BF16),
            pltpu.VMEM((L, C, HW), F32),
            pltpu.VMEM((ny, 3, *rows), F32),
            pltpu.VMEM((ny, 3, *rows), F32),
            pltpu.VMEM((ny, 2, *rows), F32),
            pltpu.VMEM((ny, 2, *rows), F32),
            pltpu.VMEM((2, *rows), F32),
            pltpu.VMEM((nz, 2, *rows), F32),
            pltpu.VMEM(rows, F32),
            pltpu.VMEM((nz, *rows), F32),
            pltpu.VMEM((2, *rows), F32),
            pltpu.VMEM((nx, 2, *rows), F32),
            pltpu.VMEM(rows, F32),
            pltpu.VMEM((nx, *rows), F32),
            pltpu.VMEM((2, ny, *rows), F32),
            pltpu.VMEM((2, ny, *rows), F32),
            pltpu.VMEM((2, 2, L, 3, 8, 128), F32),
            pltpu.VMEM((2, L, 3, 8, 128), F32),
            pltpu.VMEM((L, 3, 8, 128), F32),
            pltpu.VMEM((L, 3, 8, 128), F32),
            dma((4, ny)), dma((4, ny)),
            dma((2, nz)), dma((2, nz)),
            dma((2, nx)), dma((2, nx)),
            dma((L,)), dma((L,)),
            dma((L,)), dma((L,)),
        ],
        compiler_params=pltpu.CompilerParams(collective_id=0, has_side_effects=True, vmem_limit_bytes=16 << 20),
    )(
        *(
            pltpu.with_memory_space_constraint(v, pltpu.HBM)
            for v in (
                state_guess.reshape(C, HW),
                adjoint_guess.reshape(C, HW),
                conv_weight.reshape(L * C, 9 * C),
                conv_bias,
            )
        )
    )
    state_fixed, adjoint_fixed, weight_grad, bias_grad = pl.pallas_call(
        finish_kernel,
        out_shape=(
            grid,
            grid,
            jax.ShapeDtypeStruct((L, 8, 9 * C), F32),
            jax.ShapeDtypeStruct((L, 8), F32),
        ),
        in_specs=[pl.BlockSpec(memory_space=pl.ANY)] * 3,
        scratch_shapes=[
            pltpu.VMEM((L, 3, 8, 128), F32),
            pltpu.VMEM((9 * C, 384), BF16),
            dma((3,)),
        ],
        compiler_params=pltpu.CompilerParams(vmem_limit_bytes=16 << 20),
    )(*results)
    return (state_fixed[None, None], adjoint_fixed[None, None], weight_grad, bias_grad)


def solution(mesh):
    across = mesh.shape["layer"] // 32
    torus = Mesh(mesh.devices.reshape(across, 8, 4, 2, mesh.shape["dp"] // 2), (*LAYER, *DP))
    return jax.shard_map(
        local,
        mesh=torus,
        in_specs=(
            P(LAYER, DP, None, None),
            P(LAYER, DP, None, None),
            P(LAYER, None, None),
            P(LAYER, None),
        ),
        out_specs=(
            P(LAYER, DP, None, None),
            P(LAYER, DP, None, None),
            P(LAYER, DP, None),
            P(LAYER, DP),
        ),
        check_vma=False,
    )
```

```python
import jax
import jax.numpy as jnp
from jax import lax
from jax.experimental import pallas as pl
from jax.experimental.pallas import tpu as pltpu
from jax.sharding import Mesh
from jax.sharding import PartitionSpec as P

IMG = 16
HW = 256
C = 32
L = 4
ROWS = 3 * C
LAYER = ("x", "z", "y")
DP = ("h", "c")
MESH = pl.DeviceIdType.MESH
F32 = jnp.float32
BF16 = jnp.bfloat16


def shift_x(v, by):
    at = lax.broadcasted_iota(jnp.int32, v.shape, 1) & (IMG - 1)
    keep = (at < IMG - 1) if by > 0 else (at > 0)
    return jnp.where(keep, pltpu.roll(v, (-by) % HW, 1), 0.0)


def shift_y(v, by):
    at = lax.broadcasted_iota(jnp.int32, v.shape, 1)
    keep = (at < HW - IMG) if by > 0 else (at >= IMG)
    return jnp.where(keep, pltpu.roll(v, (-IMG * by) % HW, 1), 0.0)


def order_table():
    row = lax.broadcasted_iota(jnp.int32, (9 * C, 384), 0)
    col = lax.broadcasted_iota(jnp.int32, (9 * C, 384), 1)
    dy, rest = col >> 7, col & 127
    want = (rest & (C - 1)) * 9 + 3 * dy + (rest >> 5)
    return jnp.where((row == want) & (rest < ROWS), 1.0, 0.0).astype(BF16)


def column_of(row):
    eye = lax.broadcasted_iota(jnp.int32, (C, C), 0) == lax.broadcasted_iota(jnp.int32, (C, C), 1)
    return jnp.sum(jnp.where(eye, jnp.broadcast_to(row, (C, C)), 0.0), axis=1, keepdims=True)


def prepare(weights, table, mats, mats_t):
    wide = jnp.dot(weights, table, preferred_element_type=F32)
    centers = []
    pad = jnp.zeros((128 - ROWS, 128), F32)
    for n in range(L):
        part = [wide[n * C : (n + 1) * C, dy * 128 : (dy + 1) * 128] for dy in range(3)]
        full = jnp.concatenate(part + [pad], axis=0)
        mats[n] = full[:ROWS].astype(BF16)
        mats_t[n] = full.T[:ROWS].astype(BF16)
        at = lax.broadcasted_iota(jnp.int32, (C, 128), 1)
        want = lax.broadcasted_iota(jnp.int32, (C, 128), 0) + C
        centers.append(jnp.sum(jnp.where(at == want, part[1], 0.0), axis=1, keepdims=True))
    return centers


def forward_layer(state, mat, bias, center, gain):
    taps = jnp.concatenate([shift_x(state, -1), state, shift_x(state, 1)], axis=0).astype(BF16)
    prod = jnp.dot(mat[:, :ROWS], taps, preferred_element_type=F32)
    pre = shift_y(prod[:C], -1) + prod[C : 2 * C] + shift_y(prod[2 * C :], 1) + bias
    squash = jnp.tanh(pre)
    slope = 0.5 * (1.0 - squash * squash)
    return state + 0.5 * squash, gain * (1.0 + slope * center), taps, slope


def spread(dz):
    return jnp.concatenate([shift_y(dz, 1), dz, shift_y(dz, -1)], axis=0).astype(BF16)


def backward_layer(adjoint, mat_t, wide):
    prod = jnp.dot(mat_t[:, :ROWS], wide, preferred_element_type=F32)
    return adjoint + (shift_x(prod[:C], 1) + prod[C : 2 * C] + shift_x(prod[2 * C :], -1))


def exact_dot_t(x, table):
    total = None
    for _ in range(3):
        part = x.astype(BF16)
        x = x - part.astype(F32)
        term = lax.dot_general(part, table, (((1,), (1,)), ((), ())), preferred_element_type=F32)
        total = term if total is None else total + term
    return total


def finish(total, table, wg_ref, bg_ref):
    rows = jnp.concatenate([jnp.concatenate(total[n], axis=1) for n in range(L)], axis=0)
    grads = exact_dot_t(rows, table)
    eye = lax.broadcasted_iota(jnp.int32, (8, 8), 0) == lax.broadcasted_iota(jnp.int32, (8, 8), 1)
    for n in range(L):
        wg_ref[n] = grads[n * 8 : (n + 1) * 8]
        col = total[n][1][:, ROWS : ROWS + 1]
        row = jnp.sum(jnp.where(eye, jnp.broadcast_to(col, (8, 8)), 0.0), axis=0, keepdims=True)
        bg_ref[n : n + 1, :] = row


def send(src, dst, sems, slot, device):
    copy = pltpu.make_async_remote_copy(
        src_ref=src,
        dst_ref=dst,
        send_sem=sems[0].at[slot],
        recv_sem=sems[1].at[slot],
        device_id=device,
        device_id_type=MESH,
    )
    copy.start()
    return copy


def chained(gains, adds, start):
    values = [start]
    for g, r in zip(gains, adds):
        values.append(r if values[-1] is None else g * values[-1] + r)
    return values


def chosen(values, here):
    out = values[0]
    for k in range(1, len(values)):
        out = jnp.where(here == k, values[k], out)
    return out


def product(values):
    out = values[0]
    for v in values[1:]:
        out = out * v
    return out


def cycle_kernel(
    u_hbm, a_hbm, w_hbm, b_hbm,
    state_ref, adj_ref, sum_ref,
    u_ref, a_ref, w_ref, b_ref, in_sems, table,
    mats, mats_t, taps_ref, slope_ref,
    yc_out, yc_in, yr_out, yr_in, zc_out, zc_in, zr_out, zr_in, xc_out, xc_in, xr_out, xr_in,
    e_out, e_in, c_out, c_in, h_out, h_in,
    y_s, y_r, z_s, z_r, x_s, x_r, c_s, c_r, h_s, h_r,
):
    x, z, y = lax.axis_index("x"), lax.axis_index("z"), lax.axis_index("y")
    h, c = lax.axis_index("h"), lax.axis_index("c")
    nx, nz, ny = lax.axis_size("x"), lax.axis_size("z"), lax.axis_size("y")
    ys = [lax.rem(y + k, ny) for k in range(ny)]
    zs = [lax.rem(z + k, nz) for k in range(nz)]
    xs = [lax.rem(x + k, nx) for k in range(nx)]
    partners = [{"y": q} for q in ys[1:]] + [{"z": q} for q in zs[1:]] + [{"x": q} for q in xs[1:]]
    partners += [{"c": 1 - c}, {"h": 1 - h}]
    barrier = pltpu.get_barrier_semaphore()
    for who in partners:
        pl.semaphore_signal(barrier, inc=1, device_id=who, device_id_type=MESH)

    inputs = [
        pltpu.make_async_copy(src, dst, in_sems.at[k])
        for k, (src, dst) in enumerate(
            [(w_hbm, w_ref), (b_hbm, b_ref), (u_hbm, u_ref), (a_hbm, a_ref)]
        )
    ]
    for copy in inputs:
        copy.start()

    def gather(axis, here, others, out, into, sems, own):
        copies = [
            send(out if own else out.at[q], into.at[here], sems, k + 1, {axis: q})
            for k, q in enumerate(others)
        ]
        into[here] = out[...] if own else out[here]
        return copies

    def along_y(kind, out, into):
        return gather("y", y, ys[1:], out, into, (y_s.at[kind], y_r.at[kind]), False)

    def along_z(kind, out, into):
        return gather("z", z, zs[1:], out, into, (z_s.at[kind], z_r.at[kind]), True)

    def along_x(kind, out, into):
        return gather("x", x, xs[1:], out, into, (x_s.at[kind], x_r.at[kind]), True)

    def landed(copies):
        for copy in copies:
            copy.wait()

    table[...] = order_table()
    landed(inputs)
    centers = prepare(w_ref[...], table[...], mats, mats_t)
    state, gain = u_ref[...], jnp.ones((C, HW), F32)
    for n in range(L):
        bias = column_of(b_ref[n : n + 1, :])
        state, gain, taps, slope = forward_layer(state, mats[n], bias, centers[n], gain)
        taps_ref[n] = taps
        slope_ref[n] = slope
    adjoint = a_ref[...]
    for n in reversed(range(L)):
        adjoint = backward_layer(adjoint, mats_t[n], spread(adjoint * slope_ref[n]))
    me = (x * nz + z) * ny + y
    first, last = me == 0, me == nx * nz * ny - 1
    fwd = state - jnp.where(first, 0.0, gain) * u_ref[...]
    bwd = adjoint - jnp.where(last, 0.0, gain) * a_ref[...]
    gain = jnp.where(first | last, 0.0, gain)
    for q in range(ny):
        rows = slice(q * 8, q * 8 + 8)
        yc_out[q, 0] = gain[rows]
        yc_out[q, 1] = bwd[rows]
        yr_out[q] = fwd[rows]
    pl.semaphore_wait(barrier, len(partners))
    yc = along_y(0, yc_out, yc_in)
    yr = along_y(1, yr_out, yr_in)

    zero = jnp.zeros((8, HW), F32)
    landed(yc)
    gains = [yc_in[k, 0] for k in range(ny)]
    y_bwd = [yc_in[k, 1] for k in range(ny)][::-1]
    zc_out[0] = product(gains)
    zc_out[1] = chained(gains[::-1], y_bwd, None)[ny]
    zc = along_z(0, zc_out, zc_in)
    landed(yr)
    y_fwd = [yr_in[k] for k in range(ny)]
    zr_out[...] = chained(gains, y_fwd, None)[ny]

    landed(zc)
    z_gain = [zc_in[k, 0] for k in range(nz)]
    z_bwd = [zc_in[k, 1] for k in range(nz)][::-1]
    xc_out[0] = product(z_gain)
    xc_out[1] = chained(z_gain[::-1], z_bwd, None)[nz]
    xc = along_x(0, xc_out, xc_in)
    zr = along_z(1, zr_out, zr_in)

    landed(xc)
    x_gain = [xc_in[k, 0] for k in range(nx)]
    x_bwd = [xc_in[k, 1] for k in range(nx)][::-1]
    came = chosen(chained(x_gain[::-1], x_bwd, zero)[:nx][::-1], x)
    came = chosen(chained(z_gain[::-1], z_bwd, came)[:nz][::-1], z)
    fs = chained(gains[::-1], y_bwd, came)[:ny][::-1]
    for q in range(ny):
        e_out[0, q] = fs[q]
    f_copies = along_y(2, e_out.at[0], e_in.at[0])
    landed(zr)
    z_fwd = [zr_in[k] for k in range(nz)]
    xr_out[...] = chained(z_gain, z_fwd, None)[nz]
    xr = along_x(1, xr_out, xr_in)
    landed(f_copies)
    corrected = jnp.concatenate([e_in[0, q] for q in range(ny)], axis=0)
    adjoint = jnp.where(last, a_ref[...], corrected)
    adj_ref[...] = adjoint

    def state_rows():
        landed(xr)
        x_fwd = [xr_in[k] for k in range(nx)]
        came = chosen(chained(x_gain, x_fwd, zero)[:nx], x)
        came = chosen(chained(z_gain, z_fwd, came)[:nz], z)
        es = chained(gains, y_fwd, came)[:ny]
        for q in range(ny):
            e_out[1, q] = es[q]
        return along_y(3, e_out.at[1], e_in.at[1])

    lane = lax.broadcasted_iota(jnp.int32, (C, 128), 1)
    mine = {}

    def over_cores(n):
        to_core[n].wait()
        h_out[n] = c_out[c, 1 - h, n] + c_in[1 - h, n]
        mine[n] = [c_out[c, h, n, dy] + c_in[h, n, dy] for dy in range(3)]
        return send(h_out.at[n], h_in.at[n], (h_s, h_r), n, {"h": 1 - h})

    to_core, to_far = {}, {}
    for n in reversed(range(L)):
        dz = adjoint * slope_ref[n]
        wide = spread(dz)
        grad = lax.dot_general(
            wide, taps_ref[n], (((1,), (1,)), ((), ())), preferred_element_type=F32
        )
        grad = jnp.concatenate([grad, jnp.zeros((ROWS, 128 - ROWS), F32)], axis=1)
        sums = jnp.sum(dz, axis=1, keepdims=True)
        for dy in range(3):
            here = grad[dy * C : (dy + 1) * C]
            if dy == 1:
                here = jnp.where(lane == ROWS, sums, here)
            for owner in range(4):
                c_out[owner % 2, owner // 2, n, dy] = here[owner * 8 : (owner + 1) * 8]
        to_core[n] = send(
            c_out.at[1 - c, :, n], c_in.at[:, n], (c_s, c_r), n, {"c": 1 - c}
        )
        if n > 0:
            adjoint = backward_layer(adjoint, mats_t[n], wide)
        if n < L - 2:
            to_far[n + 2] = over_cores(n + 2)
    for n in (1, 0):
        to_far[n] = over_cores(n)
    e_copies = state_rows()
    landed(e_copies)
    corrected = jnp.concatenate([e_in[1, q] for q in range(ny)], axis=0)
    state_ref[...] = jnp.where(first, u_ref[...], corrected)
    for n in reversed(range(L)):
        to_far[n].wait()
        for dy in range(3):
            sum_ref[n, dy] = mine[n][dy] + h_in[n, dy]


def finish_kernel(state_ref, adj_ref, sum_ref, state_out, adj_out, wg_ref, bg_ref, sums, table, sems):
    copies = [
        pltpu.make_async_copy(src, dst, sems.at[k])
        for k, (src, dst) in enumerate(
            [(sum_ref, sums), (state_ref, state_out), (adj_ref, adj_out)]
        )
    ]
    for copy in copies:
        copy.start()
    table[...] = order_table()
    copies[0].wait()
    finish([[sums[n, dy] for dy in range(3)] for n in range(L)], table[...], wg_ref, bg_ref)
    for copy in copies[1:]:
        copy.wait()


def local(state_guess, adjoint_guess, conv_weight, conv_bias):
    grid = jax.ShapeDtypeStruct((C, HW), F32)
    nx, nz, ny = (lax.axis_size(axis) for axis in LAYER)
    dma = pltpu.SemaphoreType.DMA
    rows = (8, HW)
    results = pl.pallas_call(
        cycle_kernel,
        out_shape=(grid, grid, jax.ShapeDtypeStruct((L, 3, 8, 128), F32)),
        in_specs=[pl.BlockSpec(memory_space=pltpu.HBM)] * 4,
        out_specs=tuple([pl.BlockSpec(memory_space=pltpu.VMEM)] * 3),
        scratch_shapes=[
            pltpu.VMEM((C, HW), F32),
            pltpu.VMEM((C, HW), F32),
            pltpu.VMEM((L * C, 9 * C), BF16),
            pltpu.VMEM((L, C), F32),
            dma((4,)),
            pltpu.VMEM((9 * C, 384), BF16),
            pltpu.VMEM((L, ROWS, 128), BF16),
            pltpu.VMEM((L, ROWS, 128), BF16),
            pltpu.VMEM((L, ROWS, HW), BF16),
            pltpu.VMEM((L, C, HW), F32),
            pltpu.VMEM((ny, 2, *rows), F32),
            pltpu.VMEM((ny, 2, *rows), F32),
            pltpu.VMEM((ny, *rows), F32),
            pltpu.VMEM((ny, *rows), F32),
            pltpu.VMEM((2, *rows), F32),
            pltpu.VMEM((nz, 2, *rows), F32),
            pltpu.VMEM(rows, F32),
            pltpu.VMEM((nz, *rows), F32),
            pltpu.VMEM((2, *rows), F32),
            pltpu.VMEM((nx, 2, *rows), F32),
            pltpu.VMEM(rows, F32),
            pltpu.VMEM((nx, *rows), F32),
            pltpu.VMEM((2, ny, *rows), F32),
            pltpu.VMEM((2, ny, *rows), F32),
            pltpu.VMEM((2, 2, L, 3, 8, 128), F32),
            pltpu.VMEM((2, L, 3, 8, 128), F32),
            pltpu.VMEM((L, 3, 8, 128), F32),
            pltpu.VMEM((L, 3, 8, 128), F32),
            dma((4, ny)), dma((4, ny)),
            dma((2, nz)), dma((2, nz)),
            dma((2, nx)), dma((2, nx)),
            dma((L,)), dma((L,)),
            dma((L,)), dma((L,)),
        ],
        compiler_params=pltpu.CompilerParams(collective_id=0, has_side_effects=True, vmem_limit_bytes=16 << 20),
    )(
        *(
            pltpu.with_memory_space_constraint(v, pltpu.HBM)
            for v in (
                state_guess.reshape(C, HW),
                adjoint_guess.reshape(C, HW),
                conv_weight.reshape(L * C, 9 * C),
                conv_bias,
            )
        )
    )
    state_fixed, adjoint_fixed, weight_grad, bias_grad = pl.pallas_call(
        finish_kernel,
        out_shape=(
            grid,
            grid,
            jax.ShapeDtypeStruct((L, 8, 9 * C), F32),
            jax.ShapeDtypeStruct((L, 8), F32),
        ),
        in_specs=[pl.BlockSpec(memory_space=pl.ANY)] * 3,
        scratch_shapes=[
            pltpu.VMEM((L, 3, 8, 128), F32),
            pltpu.VMEM((9 * C, 384), BF16),
            dma((3,)),
        ],
        compiler_params=pltpu.CompilerParams(vmem_limit_bytes=16 << 20),
    )(*results)
    return (state_fixed[None, None], adjoint_fixed[None, None], weight_grad, bias_grad)


def solution(mesh):
    across = mesh.shape["layer"] // 32
    torus = Mesh(mesh.devices.reshape(across, 8, 4, 2, mesh.shape["dp"] // 2), (*LAYER, *DP))
    return jax.shard_map(
        local,
        mesh=torus,
        in_specs=(
            P(LAYER, DP, None, None),
            P(LAYER, DP, None, None),
            P(LAYER, None, None),
            P(LAYER, None),
        ),
        out_specs=(
            P(LAYER, DP, None, None),
            P(LAYER, DP, None, None),
            P(LAYER, DP, None),
            P(LAYER, DP),
        ),
        check_vma=False,
    )
```

```python
import jax
import jax.numpy as jnp
from jax import lax
from jax.experimental import pallas as pl
from jax.experimental.pallas import tpu as pltpu
from jax.sharding import Mesh
from jax.sharding import PartitionSpec as P

IMG = 16
HW = 256
C = 32
L = 4
ROWS = 3 * C
LAYER = ("x", "z", "y")
DP = ("h", "c")
MESH = pl.DeviceIdType.MESH
F32 = jnp.float32
BF16 = jnp.bfloat16


def shift_x(v, by):
    at = lax.broadcasted_iota(jnp.int32, v.shape, 1) & (IMG - 1)
    keep = (at < IMG - 1) if by > 0 else (at > 0)
    return jnp.where(keep, pltpu.roll(v, (-by) % HW, 1), 0.0)


def shift_y(v, by):
    at = lax.broadcasted_iota(jnp.int32, v.shape, 1)
    keep = (at < HW - IMG) if by > 0 else (at >= IMG)
    return jnp.where(keep, pltpu.roll(v, (-IMG * by) % HW, 1), 0.0)


def order_table():
    row = lax.broadcasted_iota(jnp.int32, (9 * C, 384), 0)
    col = lax.broadcasted_iota(jnp.int32, (9 * C, 384), 1)
    dy, rest = col >> 7, col & 127
    want = (rest & (C - 1)) * 9 + 3 * dy + (rest >> 5)
    return jnp.where((row == want) & (rest < ROWS), 1.0, 0.0).astype(BF16)


def order_table_t():
    row = lax.broadcasted_iota(jnp.int32, (384, 9 * C), 0)
    col = lax.broadcasted_iota(jnp.int32, (384, 9 * C), 1)
    dy, rest = row >> 7, row & 127
    want = (rest & (C - 1)) * 9 + 3 * dy + (rest >> 5)
    return jnp.where((col == want) & (rest < ROWS), 1.0, 0.0).astype(BF16)


def column_of(row):
    eye = lax.broadcasted_iota(jnp.int32, (C, C), 0) == lax.broadcasted_iota(jnp.int32, (C, C), 1)
    return jnp.sum(jnp.where(eye, jnp.broadcast_to(row, (C, C)), 0.0), axis=1, keepdims=True)


def prepare(weights, table, mats, mats_t):
    wide = jnp.dot(weights, table, preferred_element_type=F32)
    centers = []
    pad = jnp.zeros((128 - ROWS, 128), F32)
    for n in range(L):
        part = [wide[n * C : (n + 1) * C, dy * 128 : (dy + 1) * 128] for dy in range(3)]
        full = jnp.concatenate(part + [pad], axis=0)
        mats[n] = full[:ROWS].astype(BF16)
        mats_t[n] = full.T[:ROWS].astype(BF16)
        at = lax.broadcasted_iota(jnp.int32, (C, 128), 1)
        want = lax.broadcasted_iota(jnp.int32, (C, 128), 0) + C
        centers.append(jnp.sum(jnp.where(at == want, part[1], 0.0), axis=1, keepdims=True))
    return centers


def forward_layer(state, mat, bias, center, gain):
    taps = jnp.concatenate([shift_x(state, -1), state, shift_x(state, 1)], axis=0).astype(BF16)
    prod = jnp.dot(mat[:, :ROWS], taps, preferred_element_type=F32)
    pre = shift_y(prod[:C], -1) + prod[C : 2 * C] + shift_y(prod[2 * C :], 1) + bias
    squash = jnp.tanh(pre)
    slope = 0.5 * (1.0 - squash * squash)
    return state + 0.5 * squash, gain * (1.0 + slope * center), taps, slope


def spread(dz):
    return jnp.concatenate([shift_y(dz, 1), dz, shift_y(dz, -1)], axis=0).astype(BF16)


def backward_layer(adjoint, mat_t, wide):
    prod = jnp.dot(mat_t[:, :ROWS], wide, preferred_element_type=F32)
    return adjoint + (shift_x(prod[:C], 1) + prod[C : 2 * C] + shift_x(prod[2 * C :], -1))


def exact_dot(x, table):
    total = None
    for _ in range(3):
        part = x.astype(BF16)
        x = x - part.astype(F32)
        term = jnp.dot(part, table, preferred_element_type=F32)
        total = term if total is None else total + term
    return total


def finish(total, table, wg_ref, bg_ref):
    rows = jnp.concatenate([jnp.concatenate(total[n], axis=1) for n in range(L)], axis=0)
    grads = exact_dot(rows, table)
    eye = lax.broadcasted_iota(jnp.int32, (8, 8), 0) == lax.broadcasted_iota(jnp.int32, (8, 8), 1)
    for n in range(L):
        wg_ref[n] = grads[n * 8 : (n + 1) * 8]
        col = total[n][1][:, ROWS : ROWS + 1]
        row = jnp.sum(jnp.where(eye, jnp.broadcast_to(col, (8, 8)), 0.0), axis=0, keepdims=True)
        bg_ref[n : n + 1, :] = row


def send(src, dst, sems, slot, device):
    copy = pltpu.make_async_remote_copy(
        src_ref=src,
        dst_ref=dst,
        send_sem=sems[0].at[slot],
        recv_sem=sems[1].at[slot],
        device_id=device,
        device_id_type=MESH,
    )
    copy.start()
    return copy


def chained(gains, adds, start):
    values = [start]
    for g, r in zip(gains, adds):
        values.append(r if values[-1] is None else g * values[-1] + r)
    return values


def chosen(values, here):
    out = values[0]
    for k in range(1, len(values)):
        out = jnp.where(here == k, values[k], out)
    return out


def product(values):
    out = values[0]
    for v in values[1:]:
        out = out * v
    return out


def cycle_kernel(
    u_hbm, a_hbm, w_hbm, b_hbm,
    state_ref, adj_ref, sum_ref,
    u_ref, a_ref, w_ref, b_ref, in_sems, table,
    mats, mats_t, taps_ref, slope_ref,
    yc_out, yc_in, yr_out, yr_in, zc_out, zc_in, zr_out, zr_in, xc_out, xc_in, xr_out, xr_in,
    e_out, e_in, c_out, c_in, h_out, h_in,
    y_s, y_r, z_s, z_r, x_s, x_r, c_s, c_r, h_s, h_r,
):
    x, z, y = lax.axis_index("x"), lax.axis_index("z"), lax.axis_index("y")
    h, c = lax.axis_index("h"), lax.axis_index("c")
    nx, nz, ny = lax.axis_size("x"), lax.axis_size("z"), lax.axis_size("y")
    ys = [lax.rem(y + k, ny) for k in range(ny)]
    zs = [lax.rem(z + k, nz) for k in range(nz)]
    xs = [lax.rem(x + k, nx) for k in range(nx)]
    partners = [{"y": q} for q in ys[1:]] + [{"z": q} for q in zs[1:]] + [{"x": q} for q in xs[1:]]
    partners += [{"c": 1 - c}, {"h": 1 - h}]
    barrier = pltpu.get_barrier_semaphore()
    for who in partners:
        pl.semaphore_signal(barrier, inc=1, device_id=who, device_id_type=MESH)

    inputs = [
        pltpu.make_async_copy(src, dst, in_sems.at[k])
        for k, (src, dst) in enumerate(
            [(w_hbm, w_ref), (b_hbm, b_ref), (u_hbm, u_ref), (a_hbm, a_ref)]
        )
    ]
    for copy in inputs:
        copy.start()

    def gather(axis, here, others, out, into, sems, own):
        copies = [
            send(out if own else out.at[q], into.at[here], sems, k + 1, {axis: q})
            for k, q in enumerate(others)
        ]
        into[here] = out[...] if own else out[here]
        return copies

    def along_y(kind, out, into):
        return gather("y", y, ys[1:], out, into, (y_s.at[kind], y_r.at[kind]), False)

    def along_z(kind, out, into):
        return gather("z", z, zs[1:], out, into, (z_s.at[kind], z_r.at[kind]), True)

    def along_x(kind, out, into):
        return gather("x", x, xs[1:], out, into, (x_s.at[kind], x_r.at[kind]), True)

    def landed(copies):
        for copy in copies:
            copy.wait()

    table[...] = order_table()
    landed(inputs)
    centers = prepare(w_ref[...], table[...], mats, mats_t)
    state, gain = u_ref[...], jnp.ones((C, HW), F32)
    for n in range(L):
        bias = column_of(b_ref[n : n + 1, :])
        state, gain, taps, slope = forward_layer(state, mats[n], bias, centers[n], gain)
        taps_ref[n] = taps
        slope_ref[n] = slope
    adjoint = a_ref[...]
    for n in reversed(range(L)):
        adjoint = backward_layer(adjoint, mats_t[n], spread(adjoint * slope_ref[n]))
    me = (x * nz + z) * ny + y
    first, last = me == 0, me == nx * nz * ny - 1
    fwd = state - jnp.where(first, 0.0, gain) * u_ref[...]
    bwd = adjoint - jnp.where(last, 0.0, gain) * a_ref[...]
    gain = jnp.where(first | last, 0.0, gain)
    for q in range(ny):
        rows = slice(q * 8, q * 8 + 8)
        yc_out[q, 0] = gain[rows]
        yc_out[q, 1] = bwd[rows]
        yr_out[q] = fwd[rows]
    pl.semaphore_wait(barrier, len(partners))
    yc = along_y(0, yc_out, yc_in)
    yr = along_y(1, yr_out, yr_in)

    zero = jnp.zeros((8, HW), F32)
    landed(yc)
    gains = [yc_in[k, 0] for k in range(ny)]
    y_bwd = [yc_in[k, 1] for k in range(ny)][::-1]
    zc_out[0] = product(gains)
    zc_out[1] = chained(gains[::-1], y_bwd, None)[ny]
    zc = along_z(0, zc_out, zc_in)
    landed(yr)
    y_fwd = [yr_in[k] for k in range(ny)]
    zr_out[...] = chained(gains, y_fwd, None)[ny]

    landed(zc)
    z_gain = [zc_in[k, 0] for k in range(nz)]
    z_bwd = [zc_in[k, 1] for k in range(nz)][::-1]
    xc_out[0] = product(z_gain)
    xc_out[1] = chained(z_gain[::-1], z_bwd, None)[nz]
    xc = along_x(0, xc_out, xc_in)
    zr = along_z(1, zr_out, zr_in)

    landed(xc)
    x_gain = [xc_in[k, 0] for k in range(nx)]
    x_bwd = [xc_in[k, 1] for k in range(nx)][::-1]
    came = chosen(chained(x_gain[::-1], x_bwd, zero)[:nx][::-1], x)
    came = chosen(chained(z_gain[::-1], z_bwd, came)[:nz][::-1], z)
    fs = chained(gains[::-1], y_bwd, came)[:ny][::-1]
    for q in range(ny):
        e_out[0, q] = fs[q]
    f_copies = along_y(2, e_out.at[0], e_in.at[0])
    landed(zr)
    z_fwd = [zr_in[k] for k in range(nz)]
    xr_out[...] = chained(z_gain, z_fwd, None)[nz]
    xr = along_x(1, xr_out, xr_in)
    landed(f_copies)
    corrected = jnp.concatenate([e_in[0, q] for q in range(ny)], axis=0)
    adjoint = jnp.where(last, a_ref[...], corrected)
    adj_ref[...] = adjoint

    def state_rows():
        landed(xr)
        x_fwd = [xr_in[k] for k in range(nx)]
        came = chosen(chained(x_gain, x_fwd, zero)[:nx], x)
        came = chosen(chained(z_gain, z_fwd, came)[:nz], z)
        es = chained(gains, y_fwd, came)[:ny]
        for q in range(ny):
            e_out[1, q] = es[q]
        return along_y(3, e_out.at[1], e_in.at[1])

    lane = lax.broadcasted_iota(jnp.int32, (C, 128), 1)
    mine = {}

    def over_cores(n):
        to_core[n].wait()
        h_out[n] = c_out[c, 1 - h, n] + c_in[1 - h, n]
        mine[n] = [c_out[c, h, n, dy] + c_in[h, n, dy] for dy in range(3)]
        return send(h_out.at[n], h_in.at[n], (h_s, h_r), n, {"h": 1 - h})

    to_core, to_far = {}, {}
    for n in reversed(range(L)):
        dz = adjoint * slope_ref[n]
        wide = spread(dz)
        grad = lax.dot_general(
            wide, taps_ref[n], (((1,), (1,)), ((), ())), preferred_element_type=F32
        )
        grad = jnp.concatenate([grad, jnp.zeros((ROWS, 128 - ROWS), F32)], axis=1)
        sums = jnp.sum(dz, axis=1, keepdims=True)
        for dy in range(3):
            here = grad[dy * C : (dy + 1) * C]
            if dy == 1:
                here = jnp.where(lane == ROWS, sums, here)
            for owner in range(4):
                c_out[owner % 2, owner // 2, n, dy] = here[owner * 8 : (owner + 1) * 8]
        to_core[n] = send(
            c_out.at[1 - c, :, n], c_in.at[:, n], (c_s, c_r), n, {"c": 1 - c}
        )
        if n > 0:
            adjoint = backward_layer(adjoint, mats_t[n], wide)
        if n < L - 2:
            to_far[n + 2] = over_cores(n + 2)
    for n in (1, 0):
        to_far[n] = over_cores(n)
    e_copies = state_rows()
    landed(e_copies)
    corrected = jnp.concatenate([e_in[1, q] for q in range(ny)], axis=0)
    state_ref[...] = jnp.where(first, u_ref[...], corrected)
    for n in reversed(range(L)):
        to_far[n].wait()
        for dy in range(3):
            sum_ref[n, dy] = mine[n][dy] + h_in[n, dy]


def finish_kernel(state_ref, adj_ref, sum_ref, state_out, adj_out, wg_ref, bg_ref, sums, table, sems):
    copies = [
        pltpu.make_async_copy(src, dst, sems.at[k])
        for k, (src, dst) in enumerate(
            [(sum_ref, sums), (state_ref, state_out), (adj_ref, adj_out)]
        )
    ]
    for copy in copies:
        copy.start()
    table[...] = order_table_t()
    copies[0].wait()
    finish([[sums[n, dy] for dy in range(3)] for n in range(L)], table[...], wg_ref, bg_ref)
    for copy in copies[1:]:
        copy.wait()


def local(state_guess, adjoint_guess, conv_weight, conv_bias):
    grid = jax.ShapeDtypeStruct((C, HW), F32)
    nx, nz, ny = (lax.axis_size(axis) for axis in LAYER)
    dma = pltpu.SemaphoreType.DMA
    rows = (8, HW)
    results = pl.pallas_call(
        cycle_kernel,
        out_shape=(grid, grid, jax.ShapeDtypeStruct((L, 3, 8, 128), F32)),
        in_specs=[pl.BlockSpec(memory_space=pltpu.HBM)] * 4,
        out_specs=tuple([pl.BlockSpec(memory_space=pltpu.VMEM)] * 3),
        scratch_shapes=[
            pltpu.VMEM((C, HW), F32),
            pltpu.VMEM((C, HW), F32),
            pltpu.VMEM((L * C, 9 * C), BF16),
            pltpu.VMEM((L, C), F32),
            dma((4,)),
            pltpu.VMEM((9 * C, 384), BF16),
            pltpu.VMEM((L, ROWS, 128), BF16),
            pltpu.VMEM((L, ROWS, 128), BF16),
            pltpu.VMEM((L, ROWS, HW), BF16),
            pltpu.VMEM((L, C, HW), F32),
            pltpu.VMEM((ny, 2, *rows), F32),
            pltpu.VMEM((ny, 2, *rows), F32),
            pltpu.VMEM((ny, *rows), F32),
            pltpu.VMEM((ny, *rows), F32),
            pltpu.VMEM((2, *rows), F32),
            pltpu.VMEM((nz, 2, *rows), F32),
            pltpu.VMEM(rows, F32),
            pltpu.VMEM((nz, *rows), F32),
            pltpu.VMEM((2, *rows), F32),
            pltpu.VMEM((nx, 2, *rows), F32),
            pltpu.VMEM(rows, F32),
            pltpu.VMEM((nx, *rows), F32),
            pltpu.VMEM((2, ny, *rows), F32),
            pltpu.VMEM((2, ny, *rows), F32),
            pltpu.VMEM((2, 2, L, 3, 8, 128), F32),
            pltpu.VMEM((2, L, 3, 8, 128), F32),
            pltpu.VMEM((L, 3, 8, 128), F32),
            pltpu.VMEM((L, 3, 8, 128), F32),
            dma((4, ny)), dma((4, ny)),
            dma((2, nz)), dma((2, nz)),
            dma((2, nx)), dma((2, nx)),
            dma((L,)), dma((L,)),
            dma((L,)), dma((L,)),
        ],
        compiler_params=pltpu.CompilerParams(collective_id=0, has_side_effects=True, vmem_limit_bytes=16 << 20),
    )(
        *(
            pltpu.with_memory_space_constraint(v, pltpu.HBM)
            for v in (
                state_guess.reshape(C, HW),
                adjoint_guess.reshape(C, HW),
                conv_weight.reshape(L * C, 9 * C),
                conv_bias,
            )
        )
    )
    state_fixed, adjoint_fixed, weight_grad, bias_grad = pl.pallas_call(
        finish_kernel,
        out_shape=(
            grid,
            grid,
            jax.ShapeDtypeStruct((L, 8, 9 * C), F32),
            jax.ShapeDtypeStruct((L, 8), F32),
        ),
        in_specs=[pl.BlockSpec(memory_space=pl.ANY)] * 3,
        scratch_shapes=[
            pltpu.VMEM((L, 3, 8, 128), F32),
            pltpu.VMEM((384, 9 * C), BF16),
            dma((3,)),
        ],
        compiler_params=pltpu.CompilerParams(vmem_limit_bytes=16 << 20),
    )(*results)
    return (state_fixed[None, None], adjoint_fixed[None, None], weight_grad, bias_grad)


def solution(mesh):
    across = mesh.shape["layer"] // 32
    torus = Mesh(mesh.devices.reshape(across, 8, 4, 2, mesh.shape["dp"] // 2), (*LAYER, *DP))
    return jax.shard_map(
        local,
        mesh=torus,
        in_specs=(
            P(LAYER, DP, None, None),
            P(LAYER, DP, None, None),
            P(LAYER, None, None),
            P(LAYER, None),
        ),
        out_specs=(
            P(LAYER, DP, None, None),
            P(LAYER, DP, None, None),
            P(LAYER, DP, None),
            P(LAYER, DP),
        ),
        check_vma=False,
    )
```
